256 devices in a mesh: gz: 8 (over x, y_hi), xy: 32 (over z, y_lo, core).
Axes of the slice: x: 4, y: 4 (y_hi: 2, y_lo: 2; y = y_hi * 2 + y_lo), z: 8, core: 2. Of those that a mesh axis runs over, the one named last changes fastest.
Arguments:
- positions: float32 [3, 8, 32, 128], P(None, 'gz', 'xy'), may hold values from 0 to 1
- features: bfloat16 [128, 8, 32, 128], P(None, 'gz', 'xy'), may hold values from -6 to 6
- cell_counts: int32 [8, 32], P('gz', 'xy'), may hold values from 32 to 128, as said below
- radial_weights: float32 [8, 128], replicated, may hold values from -0.75 to 0.75
- mix_weights: bfloat16 [128, 128], replicated, may hold values from -0.5 to 0.5
- out_weights: float32 [128], replicated, may hold values from -0.6 to 0.6
- charge_weights: float32 [128], replicated, may hold values from -0.5 to 0.5
- spline_base: int32 [3, 8, 32, 128], P(None, 'gz', 'xy'), may hold values from 0 to 255, as said below
- spline_weights: float32 [3, 4, 8, 32, 128], P(None, None, 'gz', 'xy'), may hold values from 0 to 0.5
- spline_slopes: float32 [3, 4, 8, 32, 128], P(None, None, 'gz', 'xy'), may hold values from -2.25 to 2.25, as said below
Outputs:
- energy_atom: float32 [8, 32, 128], P('gz', 'xy')
- forces: float32 [3, 8, 32, 128], P(None, 'gz', 'xy')
The draws below stay inside these ranges and needn't reach their ends.
Inputs may be any that keep to these rules, and one draw needn't show every extreme that they name: Slots 0 to cell_counts - 1 of a cell hold atoms and the other slots are padding; some cell holds 128 atoms. For an atom of cell (cz, cx), spline_base[0] lies in cz * 16 to (cz + 1) * 16 - 1 and spline_base[1] in cx * 8 to (cx + 1) * 8 - 1; spline_base[2] lies in 0 to 255. `spline_slopes`: for each atom and each dimension the four slopes sum to zero.
All inputs are finite; a program needn't handle non-finite values.
Results may differ from the reference program's by a relative error of at most 0.003.
Values sent between devices are 32-bit elements; how exact they have to be, the bound alone decides.
A program may use at most 128 MiB of HBM per device.

```python
import jax
import jax.numpy as jnp
from jax import lax

F = 128
K = 8
TILE = 128
MZ = 128
MX = 256
MY = 256
NCZ = 8
NCX = 32


def draw_cell_counts(key, part):
    first_key, second_key = jax.random.split(jax.random.fold_in(key, 11))
    filled = jax.random.randint(first_key, (NCZ * NCX,), TILE // 4, TILE + 1)
    chosen = jax.random.randint(second_key, (), 0, NCZ * NCX)
    filled = jnp.where(jnp.arange(NCZ * NCX) == chosen, TILE, filled)
    return filled.reshape(NCZ, NCX).astype(jnp.int32)


def draw_spline_base(key, part):
    subkeys = jax.random.split(jax.random.fold_in(key, 23), 3)
    per_z = MZ // NCZ
    per_x = MX // NCX
    cell_z = jnp.arange(NCZ)[:, None, None]
    cell_x = jnp.arange(NCX)[None, :, None]
    base_z = cell_z * per_z + jax.random.randint(subkeys[0], (NCZ, NCX, TILE), 0, per_z)
    base_x = cell_x * per_x + jax.random.randint(subkeys[1], (NCZ, NCX, TILE), 0, per_x)
    base_y = jax.random.randint(subkeys[2], (NCZ, NCX, TILE), 0, MY)
    return jnp.stack([base_z, base_x, base_y], axis=0).astype(jnp.int32)


def draw_spline_slopes(key, part):
    slope_key = jax.random.fold_in(key, 37)
    shape = (3, 4, NCZ, NCX, TILE)
    raw = jnp.clip(0.5 * jax.random.normal(slope_key, shape, jnp.float32), -1.5, 1.5)
    centred = raw - jnp.mean(raw, axis=1, keepdims=True)
    return centred.astype(jnp.float32)


def levels(rng, shape, pieces, least, largest):
    factor_of, own = 1.0, jax.random.fold_in(rng, 6)
    for position, parts in pieces:
        steps = jnp.exp(jax.random.uniform(jax.random.fold_in(own, position), (parts,), jnp.float32, least / len(pieces), largest / len(pieces)))
        factor_of = factor_of * jnp.repeat(steps, shape[position] // parts).reshape([-1 if axis == position else 1 for axis in range(len(shape))])
    return factor_of


def normal_values(rng, shape, spread, most, pieces=(), kind=jnp.bfloat16):
    level = levels(rng, shape, pieces, -0.22, 0.18) if pieces else 1.0
    values = jax.random.normal(rng, shape, jnp.float32) * spread * level
    return jnp.minimum(jnp.maximum(values, -most), most).astype(kind)


def setup_inputs(seed: int = 0) -> dict:
    streams_of = jax.random.split(jax.random.key(seed), 11)
    positions = jnp.clip(1.0 * jax.random.uniform(streams_of[0], (3, NCZ, NCX, TILE), jnp.float32) ** levels(streams_of[0], (3, NCZ, NCX, TILE), ((1, 8), (2, 32)), -0.2, 0.2), 0.0, 1.0)
    features = normal_values(streams_of[1], (F, NCZ, NCX, TILE), 1.0, 6.0, ((1, 8), (2, 32)))
    cell_counts = draw_cell_counts(jax.random.fold_in(streams_of[10], 71), 0)
    radial_weights = normal_values(streams_of[3], (K, F), 0.125, 0.75, (), jnp.float32)
    mix_weights = normal_values(streams_of[4], (F, F), F ** -0.5, 0.5)
    out_weights = normal_values(streams_of[5], (F,), 0.1, 0.6, (), jnp.float32)
    charge_weights = normal_values(streams_of[6], (F,), F ** -0.5, 0.5, (), jnp.float32)
    spline_base = draw_spline_base(jax.random.fold_in(streams_of[10], 71), 0)
    spline_weights = jnp.clip(0.5 * jax.random.uniform(streams_of[8], (3, 4, NCZ, NCX, TILE), jnp.float32) ** levels(streams_of[8], (3, 4, NCZ, NCX, TILE), ((2, 8), (3, 32)), -0.2, 0.2), 0.0, 0.5)
    spline_slopes = draw_spline_slopes(jax.random.fold_in(streams_of[10], 71), 0)
    return dict(positions=positions, features=features, cell_counts=cell_counts, radial_weights=radial_weights, mix_weights=mix_weights, out_weights=out_weights, charge_weights=charge_weights, spline_base=spline_base, spline_weights=spline_weights, spline_slopes=spline_slopes)


EDGE_LEN = 6.0
PERIOD_Y = 36.0
CUTOFF = 6.0
SOFTEN = 0.04
EWALD_BETA = 8.0
COULOMB = 4.0
NEIGHBOUR_SHIFTS = [(shift_z, shift_x) for shift_z in (-1, 0, 1) for shift_x in (-1, 0, 1)]

def pair_matrix(displace):
    radius_sq = lax.optimization_barrier(jnp.sum(displace * displace, axis=0))
    radius = jnp.sqrt(radius_sq + SOFTEN)
    envelope = jnp.maximum(1.0 - radius_sq / (CUTOFF * CUTOFF), 0.0) ** 2
    orders = jnp.arange(1, K + 1).astype(jnp.float32).reshape((K,) + (1,) * radius.ndim)
    bessel = jnp.sin(orders * (jnp.pi / CUTOFF) * radius[None]) / radius[None] * envelope[None]
    direction = displace / radius[None]
    return jnp.concatenate([bessel[None], bessel[None] * direction[:, None]], axis=0)

def displacement(own_pos, near_pos, shift_z, shift_x):
    delta_z = (shift_z + near_pos[0][:, None, :] - own_pos[0][:, :, None]) * EDGE_LEN
    delta_x = (shift_x + near_pos[1][:, None, :] - own_pos[1][:, :, None]) * EDGE_LEN
    delta_y = near_pos[2][:, None, :] - own_pos[2][:, :, None]
    delta_y = jnp.where(delta_y > 0.5, delta_y - 1.0, jnp.where(delta_y < -0.5, delta_y + 1.0, delta_y)) * PERIOD_Y
    return jnp.stack([delta_z, delta_x, delta_y], axis=0)

def self_mask(shift_z, shift_x, tile_len):
    if shift_z == 0 and shift_x == 0:
        return 1.0 - jnp.eye(tile_len, dtype=jnp.float32)
    return jnp.ones((tile_len, tile_len), jnp.float32)

def readout(message, valid_rows, mix_weights, out_weights):
    invariant = (message[0] + lax.optimization_barrier(jnp.sum(message[1:] * message[1:], axis=0))).astype(jnp.bfloat16)
    cell_count, tile_len, feat_width = invariant.shape
    pre_act = jnp.dot(invariant.reshape(cell_count * tile_len, feat_width), mix_weights, preferred_element_type=jnp.float32)
    sigmoid_pre = jax.nn.sigmoid(pre_act)
    energy = lax.optimization_barrier(jnp.sum(pre_act * sigmoid_pre * out_weights, axis=-1)).reshape(cell_count, tile_len)
    slope_act = sigmoid_pre + pre_act * sigmoid_pre * (1.0 - sigmoid_pre)
    grad_pre = (slope_act * out_weights * valid_rows.reshape(-1, 1)).astype(jnp.bfloat16)
    grad_inv = jnp.dot(grad_pre, mix_weights.T, preferred_element_type=jnp.float32).reshape(cell_count, tile_len, feat_width)
    grad_msg = jnp.concatenate([grad_inv[None], 2.0 * message[1:] * grad_inv[None]], axis=0).astype(jnp.bfloat16)
    return (energy, grad_msg)

def signed_freq(freq, length):
    return (freq - length * (2 * freq >= length)).astype(jnp.float32)

def green_values(wave_z, wave_x, wave_y, len_z, len_x):
    wave_sq = (wave_z / len_z) ** 2 + (wave_x / len_x) ** 2 + (wave_y / PERIOD_Y) ** 2
    positive = wave_sq > 0
    safe_sq = jnp.where(positive, wave_sq, 1.0)
    scaled = COULOMB * jnp.exp(-jnp.pi ** 2 * safe_sq / EWALD_BETA ** 2) / (jnp.pi * len_z * len_x * PERIOD_Y * safe_sq)
    return jnp.where(positive, scaled, 0.0)

def reference(positions, features, cell_counts, radial_weights, mix_weights, out_weights, charge_weights, spline_base, spline_weights, spline_slopes):
    rows_z, rows_x, tile_len = (positions.shape[1], positions.shape[2], positions.shape[3])
    feat_width = features.shape[0]
    valid_mask = (jnp.arange(tile_len)[None, None, :] < cell_counts[:, :, None]).astype(jnp.float32)
    feat_valid = features.astype(jnp.float32) * valid_mask[None]
    charge = lax.optimization_barrier(jnp.sum(feat_valid * charge_weights[:, None, None, None], axis=0))
    radial = (jnp.transpose(feat_valid, (1, 2, 3, 0))[None] * radial_weights[:, None, None, None, :]).astype(jnp.bfloat16)

    def row_step(force_acc, row_index):
        own_pos = positions[:, row_index]
        message = jnp.zeros((4, rows_x, tile_len, feat_width), jnp.float32)
        for shift_z, shift_x in NEIGHBOUR_SHIFTS:
            near_row = (row_index + shift_z) % rows_z
            near_pos = jnp.roll(positions[:, near_row], -shift_x, axis=1)
            near_radial = jnp.roll(radial[:, near_row], -shift_x, axis=1).astype(jnp.float32)
            displace = displacement(own_pos, near_pos, shift_z, shift_x)
            pair_values = (pair_matrix(displace) * self_mask(shift_z, shift_x, tile_len)).astype(jnp.bfloat16)
            message = message + jnp.einsum('cknij,knjf->cnif', pair_values.astype(jnp.float32), near_radial, precision=lax.Precision.HIGHEST)
        energy, grad_msg = readout(message, valid_mask[row_index], mix_weights, out_weights)
        grad_wide = grad_msg.astype(jnp.float32)
        own_force = jnp.zeros((3, rows_x, tile_len), jnp.float32)
        for shift_z, shift_x in NEIGHBOUR_SHIFTS:
            near_row = (row_index + shift_z) % rows_z
            near_pos = jnp.roll(positions[:, near_row], -shift_x, axis=1)
            near_radial = jnp.roll(radial[:, near_row], -shift_x, axis=1).astype(jnp.float32)
            displace = displacement(own_pos, near_pos, shift_z, shift_x)
            grad_pair = jnp.einsum('cnif,knjf->cknij', grad_wide, near_radial, precision=lax.Precision.HIGHEST) * self_mask(shift_z, shift_x, tile_len)
            pullback = jax.vjp(pair_matrix, displace)[1]
            grad_disp = pullback(grad_pair)[0]
            own_force = own_force + lax.optimization_barrier(jnp.sum(grad_disp, axis=-1))
            near_force = -lax.optimization_barrier(jnp.sum(grad_disp, axis=-2))
            force_acc = force_acc.at[:, near_row].add(jnp.roll(near_force, shift_x, axis=1))
        force_acc = force_acc.at[:, row_index].add(own_force)
        return (force_acc, energy)
    force_sr, energy_sr = lax.scan(row_step, jnp.zeros((3, rows_z, rows_x, tile_len), jnp.float32), jnp.arange(rows_z))
    spline_points = jnp.arange(4)
    point_z = (spline_base[0][..., None] - 1 + spline_points) % MZ
    point_x = (spline_base[1][..., None] - 1 + spline_points) % MX
    point_y = (spline_base[2][..., None] - 1 + spline_points) % MY
    grid_shape = point_z.shape[:-1] + (4, 4, 4)
    full_z = jnp.broadcast_to(point_z[..., :, None, None], grid_shape)
    full_x = jnp.broadcast_to(point_x[..., None, :, None], grid_shape)
    full_y = jnp.broadcast_to(point_y[..., None, None, :], grid_shape)
    weight_z = jnp.moveaxis(spline_weights[0], 0, -1)
    weight_x = jnp.moveaxis(spline_weights[1], 0, -1)
    weight_y = jnp.moveaxis(spline_weights[2], 0, -1)
    slope_z = jnp.moveaxis(spline_slopes[0], 0, -1)
    slope_x = jnp.moveaxis(spline_slopes[1], 0, -1)
    slope_y = jnp.moveaxis(spline_slopes[2], 0, -1)
    stencil = weight_z[..., :, None, None] * weight_x[..., None, :, None] * weight_y[..., None, None, :]
    charge_mesh = jnp.zeros((MZ, MX, MY), jnp.float32).at[full_z, full_x, full_y].add(charge[..., None, None, None] * stencil)
    len_z = EDGE_LEN * rows_z
    len_x = EDGE_LEN * rows_x
    green_table = green_values(signed_freq(jnp.arange(MZ), MZ)[:, None, None], signed_freq(jnp.arange(MX), MX)[None, :, None], signed_freq(jnp.arange(MY), MY)[None, None, :], len_z, len_x)
    spectrum = jnp.fft.fftn(charge_mesh)
    potential_mesh = (jnp.real(jnp.fft.ifftn(spectrum * green_table)) * (MZ * MX * MY)).astype(jnp.float32)
    at_points = potential_mesh[full_z, full_x, full_y]
    summed_axes = (-3, -2, -1)
    potential = lax.optimization_barrier(jnp.sum(stencil * at_points, axis=summed_axes))
    force_z = -charge * lax.optimization_barrier(jnp.sum(slope_z[..., :, None, None] * weight_x[..., None, :, None] * weight_y[..., None, None, :] * at_points, axis=summed_axes))
    force_x = -charge * lax.optimization_barrier(jnp.sum(weight_z[..., :, None, None] * slope_x[..., None, :, None] * weight_y[..., None, None, :] * at_points, axis=summed_axes))
    force_y = -charge * lax.optimization_barrier(jnp.sum(weight_z[..., :, None, None] * weight_x[..., None, :, None] * slope_y[..., None, None, :] * at_points, axis=summed_axes))
    energy_atom = valid_mask * (energy_sr + 0.5 * charge * potential)
    forces = force_sr + jnp.stack([force_z, force_x, force_y], axis=0)
    return (energy_atom, forces)
```

```python
import functools

import jax
import jax.numpy as jnp
import numpy as np
from jax import lax
from jax.experimental import pallas as pl
from jax.experimental.pallas import tpu as pltpu
from jax.sharding import PartitionSpec as P

MESH = pl.DeviceIdType.MESH
F32 = jnp.float32
BF16 = jnp.bfloat16

K = 8
F = 128
T = 128
BZ = 16
BX = 8
EZ = BZ + 3
EX = BX + 3
ABP = 256
EDGE_LEN = 6.0
PERIOD_Y = 36.0
CUTOFF = 6.0
SOFTEN = 0.04
EWALD_BETA = 8.0
COULOMB = 4.0
JC = 32
OFFSETS = [(dz, dx) for dz in (-1, 0, 1) for dx in (-1, 0, 1)]
PAY = 136


def split_np(x):
    x = np.asarray(x, np.float32)
    hi = x.astype(jnp.bfloat16)
    lo = (x - hi.astype(np.float32)).astype(jnp.bfloat16)
    return np.stack([hi, lo])


@functools.lru_cache(None)
def tables(G, S):
    MZ, MX, MY, N = G * BZ, S * BX, G * S, G * S
    p = np.arange(MY)
    ky = np.where(p <= MY // 2, p, p - MY // 2)
    ang = 2 * np.pi * ((ky[:, None] * np.arange(MY)[None, :]) % MY) / MY
    ct = np.where((p <= MY // 2)[:, None], np.cos(ang), np.sin(ang))
    kzl = np.repeat(np.arange(G), S)
    kxl = np.tile(np.arange(S), G)
    ang = 2 * np.pi * (((kzl[:, None] * kzl[None, :]) % G) / G + ((kxl[:, None] * kxl[None, :]) % S) / S)
    w = np.concatenate([np.cos(ang), -np.sin(ang)], axis=0)
    a = np.repeat(np.arange(EZ), EX)
    b = np.tile(np.arange(EX), EZ)
    ang = 2 * np.pi * (kzl[:, None] * (a - 1)[None] / MZ + kxl[:, None] * (b - 1)[None] / MX)
    pad = ((0, 0), (0, ABP - EZ * EX))
    tw = np.stack([np.pad(np.cos(ang), pad), np.pad(-np.sin(ang), pad)]).astype(np.float32)
    kzh = np.repeat(np.arange(BZ), BX)
    kxh = np.tile(np.arange(BX), BZ)
    ang = 2 * np.pi * ((a - 1)[:, None] * kzh[None] / BZ + (b - 1)[:, None] * kxh[None] / BX)
    pad = ((0, ABP - EZ * EX), (0, 0))
    mr, mi = np.pad(np.cos(ang), pad), np.pad(-np.sin(ang), pad)
    fm = np.block([[mr, mi], [-mi, mr]])
    return split_np(ct), split_np(w), tw, split_np(fm)


def fit(fn, degree, top):
    z = top * (0.5 - 0.5 * np.cos(np.pi * (np.arange(200) + 0.5) / 200))
    return [float(c) for c in np.polynomial.polynomial.polyfit(z, fn(z), degree)]


COS_C = fit(lambda z: np.cos(np.pi * np.sqrt(z)), 6, 0.2526)
SIN_C = fit(lambda z: np.sin(np.pi * np.sqrt(z + 1e-300)) / np.sqrt(z + 1e-300), 5, 0.2526)


def poly(coefs, z):
    acc = jnp.full_like(z, coefs[-1])
    for c in coefs[-2::-1]:
        acc = acc * z + c
    return acc


def split(x):
    hi = x.astype(BF16)
    return hi, (x - hi.astype(F32)).astype(BF16)


def dg(a, b, dims):
    return lax.dot_general(a, b, (dims, ((), ())), preferred_element_type=F32)


NN = ((1,), (0,))
NT = ((1,), (1,))
TN = ((0,), (0,))


def dot3(a, b, dims):
    return dg(a[0], b[0], dims) + (dg(a[0], b[1], dims) + dg(a[1], b[0], dims))


def columns(row_block):
    return jnp.transpose(row_block)


def geometry(own, near, off_z, off_x, keep):
    dz = (off_z + near[0] - own[0]) * EDGE_LEN
    dx = (off_x + near[1] - own[1]) * EDGE_LEN
    dy = near[2] - own[2]
    dy = jnp.where(dy > 0.5, dy - 1.0, jnp.where(dy < -0.5, dy + 1.0, dy)) * PERIOD_Y
    rsq = dz * dz + dx * dx + dy * dy
    r2 = rsq + SOFTEN
    rinv = lax.rsqrt(r2)
    r = r2 * rinv
    x = jnp.minimum(r, 6.014) * (1.0 / CUTOFF) - 0.5
    z = x * x
    s1 = poly(COS_C, z)
    c1 = -x * poly(SIN_C, z)
    m = jnp.maximum(1.0 - rsq * (1.0 / (CUTOFF * CUTOFF)), 0.0)
    if keep is not None:
        m = m * keep
    env = m * m
    u = (dz * rinv, dx * rinv, dy * rinv)
    return rinv, s1, c1, m, env, u


def kernel(
    G, S,
    pos_ref, feat_ref, cnt_ref, rw_ref, mix_ref, ow_ref, cw_ref, base_ref, wts_ref, slp_ref,
    ct_hbm, w_hbm, tw_hbm, fm_hbm,
    e_out, f_out,
    ct, w, tw, fm, halo, rwb, post, pv, radf, msg, gm, gp, nf, ff, fr,
    ee, wzx, spec, plane, back, field,
    tab_sem, hs, hr, fs, fr_sem, as_, ar, bs, br, ls, phase, halo_t,
):
    N = G * S
    MY = N
    g = lax.axis_index("gz")
    s = lax.axis_index("xy")
    me = g * S + s

    def peer(dz, dx):
        return (lax.rem(g + (dz + G), G), lax.rem(s + (dx + S), S))

    bar = pltpu.get_barrier_semaphore()
    diag = [(dz, dx) for dz in (-1, 1) for dx in (-1, 1)]
    for dz, dx in diag:
        pl.semaphore_signal(bar, inc=1, device_id=peer(dz, dx), device_id_type=MESH)
    for dz in range(1, G):
        pl.semaphore_signal(bar, inc=1, device_id=peer(dz, 0), device_id_type=MESH)

    def sig_row(k, _):
        pl.semaphore_signal(bar, inc=1, device_id=(g, lax.rem(s + k, S)), device_id_type=MESH)
        return 0

    lax.fori_loop(1, S, sig_row, 0)

    tabs = [pltpu.make_async_copy(h, v, tab_sem.at[i]) for i, (h, v) in enumerate(
        [(ct_hbm, ct), (w_hbm, w), (tw_hbm, tw), (fm_hbm, fm)])]
    for t in tabs:
        t.start()

    lane = lax.broadcasted_iota(jnp.int32, (1, T), 1)
    valid = (lane < cnt_ref[0, 0]).astype(F32)
    featv = feat_ref[...].astype(F32) * valid
    halo[4, 0:F, :] = featv
    halo[4, F:F + 8, :] = jnp.concatenate([pos_ref[...], jnp.zeros((5, T), F32)], axis=0)
    cwt = columns(jnp.broadcast_to(cw_ref[...], (8, F)))
    owt = columns(jnp.broadcast_to(ow_ref[...], (8, F)))
    charge = jnp.sum(featv * cwt[:, 0:1], axis=0, keepdims=True)

    yrow = lax.broadcasted_iota(jnp.int32, (MY, T), 0)
    ty = jnp.bitwise_and(yrow - base_ref[2:3, :] + 1, MY - 1)
    wy = jnp.zeros((MY, T), F32)
    sy = jnp.zeros((MY, T), F32)
    for c in range(4):
        hit = ty == c
        wy = wy + jnp.where(hit, wts_ref[8 + c:9 + c, :], 0.0)
        sy = sy + jnp.where(hit, slp_ref[8 + c:9 + c, :], 0.0)
    ab = lax.broadcasted_iota(jnp.int32, (ABP, T), 0)
    arow = lax.shift_right_logical(ab * 373, 12)
    brow = ab - arow * EX
    tz = arow - (base_ref[0:1, :] - g * BZ)
    tx = brow - (base_ref[1:2, :] - s * BX)
    zero = jnp.zeros((ABP, T), F32)
    wz, sz, wx, sx = zero, zero, zero, zero
    for c in range(4):
        hit = tz == c
        wz = wz + jnp.where(hit, wts_ref[c:c + 1, :], 0.0)
        sz = sz + jnp.where(hit, slp_ref[c:c + 1, :], 0.0)
        hit = tx == c
        wx = wx + jnp.where(hit, wts_ref[4 + c:5 + c, :], 0.0)
        sx = sx + jnp.where(hit, slp_ref[4 + c:5 + c, :], 0.0)
    wzx[0] = wz * wx
    wzx[1] = sz * wx
    wzx[2] = wz * sx

    tabs[0].wait()
    yw = split(jnp.concatenate([wy, sy], axis=1))
    e_all = dot3((ct[0], ct[1]), yw, NN)
    eh, el = split(e_all)
    ee[0] = eh
    ee[1] = el
    spectrum = dot3((eh[:, :T], el[:, :T]), split(wzx[0] * charge), NT)
    spec[:, 0, :] = spectrum[:, :128]
    spec[:, 1, :] = spectrum[:, 128:]

    pl.semaphore_wait(bar, 4 + G - 1 + S - 1)

    def sig_phase(k, _):
        pl.semaphore_signal(phase, inc=1, device_id=(g, lax.rem(s + k, S)), device_id_type=MESH)
        return 0

    lax.fori_loop(1, S, sig_phase, 0)

    halo_copies = []
    for n, (dz, dx) in enumerate(OFFSETS):
        if n == 4:
            continue
        cp = pltpu.make_async_remote_copy(
            src_ref=halo.at[4], dst_ref=halo.at[8 - n], send_sem=hs.at[n], recv_sem=hr.at[8 - n],
            device_id=peer(dz, dx), device_id_type=MESH)
        cp.start()
        halo_copies.append(cp)

    pl.semaphore_wait(phase, S - 1)

    def exchange(src, dst, send_sem, recv_sem):
        own = pltpu.make_async_copy(src.at[me], dst.at[me], ls)
        own.start()

        def send(k, _):
            q = lax.rem(me + k, N)
            pltpu.make_async_remote_copy(
                src_ref=src.at[q], dst_ref=dst.at[me], send_sem=send_sem, recv_sem=recv_sem,
                device_id=(q // S, lax.rem(q, S)), device_id_type=MESH).start()
            return 0

        lax.fori_loop(1, N, send, 0)
        own.wait()

    def arrived(dst, sem):
        pltpu.make_async_copy(dst.at[pl.ds(0, N - 1)], dst.at[pl.ds(0, N - 1)], sem).wait()

    exchange(spec, plane, as_, ar)

    rwt = columns(rw_ref[...])
    for k in range(K):
        rwb[k] = jnp.broadcast_to(rwt[:, k:k + 1], (F, T))
    msg[...] = jnp.zeros_like(msg)
    for cp in halo_copies:
        cp.wait_recv()
    own_rows = [pos_ref[c:c + 1, :] for c in range(3)]
    lane_c = lax.broadcasted_iota(jnp.int32, (JC, T), 1)
    row_c = lax.broadcasted_iota(jnp.int32, (JC, T), 0)

    def pair_inputs(n, j0):
        near = [jnp.broadcast_to(post[n, pl.ds(j0, JC), c:c + 1], (JC, T)) for c in range(3)]
        off_z = (n // 3 - 1).astype(F32)
        off_x = (lax.rem(n, 3) - 1).astype(F32)
        same = jnp.logical_and(row_c + j0 == lane_c, n == 4)
        keep = jnp.where(same, 0.0, 1.0)
        return geometry(own_rows, near, off_z, off_x, keep)

    def forward(n, _):
        post[n] = jnp.transpose(halo[n, F:F + 8, :])
        feat = halo[n, 0:F, :]
        for k in range(K):
            radf[:, k * T:(k + 1) * T] = (feat * rwb[k]).astype(BF16)

        def chunk(t, _):
            j0 = pl.multiple_of(t * JC, JC)
            rinv, s1, c1, m, env, u = pair_inputs(n, j0)
            amp = env * rinv
            two_c = 2.0 * c1
            s_prev, s_now = jnp.zeros_like(s1), s1
            for k in range(K):
                e = s_now * amp
                rows = pl.ds(k * T + j0, JC)
                pv[rows, 0:T] = e.astype(BF16)
                for c in range(3):
                    pv[rows, (c + 1) * T:(c + 2) * T] = (e * u[c]).astype(BF16)
                s_prev, s_now = s_now, two_c * s_now - s_prev
            return 0

        lax.fori_loop(0, T // JC, chunk, 0)
        msg[...] += dg(radf[...], pv[...], NN)
        return 0

    lax.fori_loop(0, 9, forward, 0)

    m0 = msg[:, 0:T]
    mc = [msg[:, (c + 1) * T:(c + 2) * T] for c in range(3)]
    inv = (m0 + (mc[0] * mc[0] + mc[1] * mc[1] + mc[2] * mc[2])).astype(BF16)
    mix = mix_ref[...]
    pre = dg(mix, inv, TN)
    sig = 1.0 / (1.0 + jnp.exp(-pre))
    owc = owt[:, 0:1]
    energy_sr = jnp.sum(pre * sig * owc, axis=0, keepdims=True)
    grad_pre = ((sig + pre * sig * (1.0 - sig)) * owc * valid).astype(BF16)
    grad_inv = dg(mix, grad_pre, NN)
    gm[:, 0:T] = grad_inv.astype(BF16)
    for c in range(3):
        gm[:, (c + 1) * T:(c + 2) * T] = (2.0 * mc[c] * grad_inv).astype(BF16)

    for t in tabs[1:]:
        t.wait()
    arrived(plane, ar)
    rs = split(jnp.concatenate([plane[:, 0, :], plane[:, 1, :]], axis=1))
    yr = dot3((w[0, 0:N], w[1, 0:N]), rs, NN)
    yi = dot3((w[0, N:], w[1, N:]), rs, NN)
    tr, ti = tw[0], tw[1]
    yy = split(jnp.concatenate([tr * yr - ti * yi, tr * yi + ti * yr], axis=1))
    zz = dot3(yy, (fm[0], fm[1]), NN)
    kk = lax.broadcasted_iota(jnp.int32, (N, 128), 0)
    hh = lax.broadcasted_iota(jnp.int32, (N, 128), 1)
    kz = kk // S + G * (hh // BX)
    kx = lax.rem(kk, S) + S * lax.rem(hh, BX)
    mz_, mx_ = G * BZ, S * BX
    kz = (kz - mz_ * (2 * kz >= mz_).astype(jnp.int32)).astype(F32)
    kx = (kx - mx_ * (2 * kx >= mx_).astype(jnp.int32)).astype(F32)
    ky_i = jnp.where(me <= MY // 2, me, me - MY // 2)
    ky = ky_i.astype(F32)
    twice = jnp.where(jnp.logical_or(me == 0, me == MY // 2), 1.0, 2.0)
    len_z, len_x = EDGE_LEN * G, EDGE_LEN * S
    fz, fx, fy = kz * (1.0 / len_z), kx * (1.0 / len_x), ky * (1.0 / PERIOD_Y)
    wsq = fz * fz + fx * fx + fy * fy
    positive = wsq > 0
    safe = jnp.where(positive, wsq, 1.0)
    green = COULOMB * jnp.exp(safe * (-np.pi ** 2 / EWALD_BETA ** 2)) / (
        np.pi * len_z * len_x * PERIOD_Y * safe)
    green = jnp.where(positive, green * twice, 0.0)
    zs = split(zz * jnp.concatenate([green, green], axis=1))
    vv = dot3(zs, (fm[0], fm[1]), NT)
    vr, vi = vv[:, :ABP], vv[:, ABP:]
    pr = split(tr * vr + ti * vi)
    pi_ = split(tr * vi - ti * vr)
    uu = dot3((w[0, 0:N], w[1, 0:N]), pr, NN) + dot3((w[0, N:], w[1, N:]), pi_, NN)
    back[:, 0, :] = uu[:, :128]
    back[:, 1, :] = uu[:, 128:]

    exchange(back, field, bs, br)

    def backward(n, own):
        feat_t = jnp.transpose(halo[n, 0:F, :])
        halo_t[...] = feat_t

        def chunk(t, own):
            j0 = pl.multiple_of(t * JC, JC)
            ft = halo_t[pl.ds(j0, JC), :]
            rad_t = jnp.concatenate([(ft * rw_ref[k:k + 1, :]).astype(BF16) for k in range(K)], axis=0)
            gp[...] = dg(rad_t, gm[...], NN)
            rinv, s1, c1, m, env, u = pair_inputs(n, j0)
            amp = env * rinv
            damp = -(m * (1.0 / 9.0) + env * (rinv * rinv))
            two_c = 2.0 * c1
            s_prev, s_now = jnp.zeros_like(s1), s1
            c_prev, c_now = jnp.ones_like(c1), c1
            sums = [None] * 4
            kcs = [None] * 4
            for k in range(K):
                kc = c_now * float(k + 1)
                for c in range(4):
                    v = gp[k * JC:(k + 1) * JC, c * T:(c + 1) * T]
                    sums[c] = v * s_now if k == 0 else sums[c] + v * s_now
                    kcs[c] = v * kc if k == 0 else kcs[c] + v * kc
                s_prev, s_now = s_now, two_c * s_now - s_prev
                c_prev, c_now = c_now, two_c * c_now - c_prev
            ar_ = amp * rinv
            tc = [ar_ * sums[c + 1] for c in range(3)]
            s_q = sums[0] + (u[0] * sums[1] + u[1] * sums[2] + u[2] * sums[3])
            k_q = kcs[0] + (u[0] * kcs[1] + u[1] * kcs[2] + u[2] * kcs[3])
            br_ = (amp * (np.pi / CUTOFF)) * k_q + damp * s_q - (u[0] * tc[0] + u[1] * tc[1] + u[2] * tc[2])
            grads = [tc[c] + u[c] * br_ for c in range(3)]
            for c in range(3):
                nf[n, pl.ds(j0, JC), c:c + 1] = -jnp.sum(grads[c], axis=1, keepdims=True)
            return tuple(
                own[c] + sum(grads[c][i * 8:(i + 1) * 8] for i in range(JC // 8)) for c in range(3))

        own = lax.fori_loop(0, T // JC, chunk, own)
        ff[n] = jnp.transpose(nf[n])[0:8, :]
        return own

    zero8 = jnp.zeros((8, T), F32)
    nf[...] = jnp.zeros_like(nf)
    own = lax.fori_loop(0, 9, backward, (zero8, zero8, zero8))

    force_copies = []
    for n, (dz, dx) in enumerate(OFFSETS):
        if n == 4:
            continue
        cp = pltpu.make_async_remote_copy(
            src_ref=ff.at[n], dst_ref=fr.at[8 - n], send_sem=fs.at[n], recv_sem=fr_sem.at[8 - n],
            device_id=peer(dz, dx), device_id_type=MESH)
        cp.start()
        force_copies.append(cp)

    arrived(field, br)
    phi = split(jnp.concatenate([field[:, 0, :], field[:, 1, :]], axis=1))
    along = dot3(phi, (ee[0], ee[1]), TN)
    a_w, a_s = along[:, :T], along[:, T:]
    pot = jnp.sum(a_w * wzx[0], axis=0, keepdims=True)
    rec = [
        -charge * jnp.sum(a_w * wzx[1], axis=0, keepdims=True),
        -charge * jnp.sum(a_w * wzx[2], axis=0, keepdims=True),
        -charge * jnp.sum(a_s * wzx[0], axis=0, keepdims=True),
    ]
    e_out[...] = valid * (energy_sr + 0.5 * charge * pot)

    for cp in force_copies:
        cp.wait_recv()
    near = ff[4]
    for n in range(9):
        if n != 4:
            near = near + fr[n]
    for c in range(3):
        f_out[c:c + 1, :] = jnp.sum(own[c], axis=0, keepdims=True) + near[c:c + 1, :] + rec[c]

    for cp in halo_copies + force_copies:
        cp.wait_send()
    arrived(spec, as_)
    arrived(back, bs)


def local(G, S, positions, features, cell_counts, radial_weights, mix_weights, out_weights,
          charge_weights, spline_base, spline_weights, spline_slopes):
    N = G * S
    vm = pl.BlockSpec(memory_space=pltpu.VMEM)
    anys = pl.BlockSpec(memory_space=pl.ANY)
    V = pltpu.VMEM
    DMA = pltpu.SemaphoreType.DMA
    e, f = pl.pallas_call(
        functools.partial(kernel, G, S),
        out_shape=(jax.ShapeDtypeStruct((1, T), F32), jax.ShapeDtypeStruct((3, T), F32)),
        in_specs=[vm, vm, pl.BlockSpec(memory_space=pltpu.SMEM)] + [vm] * 7 + [anys] * 4,
        out_specs=[vm, vm],
        scratch_shapes=[
            V((2, N, N), BF16), V((2, 2 * N, N), BF16), V((2, N, ABP), F32), V((2, 2 * ABP, 256), BF16),
            V((9, PAY, T), F32), V((K, F, T), F32), V((9, T, 8), F32), V((K * T, 4 * T), BF16),
            V((F, K * T), BF16), V((F, 4 * T), F32), V((F, 4 * T), BF16), V((K * JC, 4 * T), F32),
            V((9, T, 128), F32), V((9, 8, T), F32), V((9, 8, T), F32),
            V((2, N, 2 * T), BF16), V((3, ABP, T), F32),
            V((N, 2, 128), F32), V((N, 2, 128), F32), V((N, 2, 128), F32), V((N, 2, 128), F32),
            DMA((4,)), DMA((9,)), DMA((9,)), DMA((9,)), DMA((9,)),
            DMA, DMA, DMA, DMA, DMA, pltpu.SemaphoreType.REGULAR,
            V((T, F), F32),
        ],
        compiler_params=pltpu.CompilerParams(collective_id=0, has_side_effects=True,
                                             vmem_limit_bytes=40 * 1024 * 1024),
    )(
        positions.reshape(3, T), features.reshape(F, T), cell_counts, radial_weights, mix_weights,
        out_weights.reshape(1, F), charge_weights.reshape(1, F), spline_base.reshape(3, T),
        spline_weights.reshape(12, T), spline_slopes.reshape(12, T),
        *[jnp.asarray(t) for t in tables(G, S)],
    )
    return e.reshape(1, 1, T), f.reshape(3, 1, 1, T)


def solution(mesh):
    placed = (
        P(None, "gz", "xy", None), P(None, "gz", "xy", None), P("gz", "xy"), P(), P(), P(), P(),
        P(None, "gz", "xy", None), P(None, None, "gz", "xy", None), P(None, None, "gz", "xy", None),
    )
    return jax.shard_map(
        functools.partial(local, mesh.shape["gz"], mesh.shape["xy"]),
        mesh=mesh, in_specs=placed,
        out_specs=(P("gz", "xy", None), P(None, "gz", "xy", None)),
        check_vma=False,
    )
```

```python
import functools

import jax
import jax.numpy as jnp
import numpy as np
from jax import lax
from jax.experimental import pallas as pl
from jax.experimental.pallas import tpu as pltpu
from jax.sharding import PartitionSpec as P

MESH = pl.DeviceIdType.MESH
F32 = jnp.float32
BF16 = jnp.bfloat16

K = 8
F = 128
T = 128
BZ = 16
BX = 8
EZ = BZ + 3
EX = BX + 3
ABP = 256
EDGE_LEN = 6.0
PERIOD_Y = 36.0
CUTOFF = 6.0
SOFTEN = 0.04
EWALD_BETA = 8.0
COULOMB = 4.0
IC = 32
OFFSETS = [(dz, dx) for dz in (-1, 0, 1) for dx in (-1, 0, 1)]


def split_np(x):
    x = np.asarray(x, np.float32)
    hi = x.astype(jnp.bfloat16)
    lo = (x - hi.astype(np.float32)).astype(jnp.bfloat16)
    return np.stack([hi, lo])


@functools.lru_cache(None)
def tables(G, S):
    MZ, MX, MY, N = G * BZ, S * BX, G * S, G * S
    p = np.arange(MY)
    ky = np.where(p <= MY // 2, p, p - MY // 2)
    ang = 2 * np.pi * ((ky[:, None] * np.arange(MY)[None, :]) % MY) / MY
    ct = np.where((p <= MY // 2)[:, None], np.cos(ang), np.sin(ang))
    kzl = np.repeat(np.arange(G), S)
    kxl = np.tile(np.arange(S), G)
    ang = 2 * np.pi * (((kzl[:, None] * kzl[None, :]) % G) / G + ((kxl[:, None] * kxl[None, :]) % S) / S)
    w = np.concatenate([np.cos(ang), -np.sin(ang)], axis=0)
    a = np.repeat(np.arange(EZ), EX)
    b = np.tile(np.arange(EX), EZ)
    ang = 2 * np.pi * (kzl[:, None] * (a - 1)[None] / MZ + kxl[:, None] * (b - 1)[None] / MX)
    pad = ((0, 0), (0, ABP - EZ * EX))
    tw = np.stack([np.pad(np.cos(ang), pad), np.pad(-np.sin(ang), pad)]).astype(np.float32)
    kzh = np.repeat(np.arange(BZ), BX)
    kxh = np.tile(np.arange(BX), BZ)
    ang = 2 * np.pi * ((a - 1)[:, None] * kzh[None] / BZ + (b - 1)[:, None] * kxh[None] / BX)
    pad = ((0, ABP - EZ * EX), (0, 0))
    mr, mi = np.pad(np.cos(ang), pad), np.pad(-np.sin(ang), pad)
    fm = np.block([[mr, mi], [-mi, mr]])
    return split_np(ct), split_np(w), tw, split_np(fm)


def fit(fn, degree, top):
    z = top * (0.5 - 0.5 * np.cos(np.pi * (np.arange(200) + 0.5) / 200))
    return [float(c) for c in np.polynomial.polynomial.polyfit(z, fn(z), degree)]


COS_C = fit(lambda z: np.cos(np.pi * np.sqrt(z)), 6, 0.2526)
SIN_C = fit(lambda z: np.sin(np.pi * np.sqrt(z + 1e-300)) / np.sqrt(z + 1e-300), 5, 0.2526)


def poly(coefs, z):
    acc = jnp.full_like(z, coefs[-1])
    for c in coefs[-2::-1]:
        acc = acc * z + c
    return acc


def split(x):
    hi = x.astype(BF16)
    return hi, (x - hi.astype(F32)).astype(BF16)


def dg(a, b, dims):
    return lax.dot_general(a, b, (dims, ((), ())), preferred_element_type=F32)


NN = ((1,), (0,))
NT = ((1,), (1,))
TN = ((0,), (0,))


def dot3(a, b, dims):
    return dg(a[0], b[0], dims) + (dg(a[0], b[1], dims) + dg(a[1], b[0], dims))


def geometry(own, near, off_z, off_x, keep):
    dz = (off_z + near[0] - own[0]) * EDGE_LEN
    dx = (off_x + near[1] - own[1]) * EDGE_LEN
    dy = near[2] - own[2]
    dy = jnp.where(dy > 0.5, dy - 1.0, jnp.where(dy < -0.5, dy + 1.0, dy)) * PERIOD_Y
    rsq = dz * dz + dx * dx + dy * dy
    r2 = rsq + SOFTEN
    rinv = lax.rsqrt(r2)
    r = r2 * rinv
    x = jnp.minimum(r, 6.014) * (1.0 / CUTOFF) - 0.5
    z = x * x
    s1 = poly(COS_C, z)
    c1 = -x * poly(SIN_C, z)
    m = jnp.maximum(1.0 - rsq * (1.0 / (CUTOFF * CUTOFF)), 0.0) * keep
    env = m * m
    u = (dz * rinv, dx * rinv, dy * rinv)
    return rinv, s1, c1, m, env, u


def kernel(
    G, S,
    pos_hbm, feat_hbm, cnt_hbm, rw_hbm, mix_hbm, ow_hbm, cw_hbm, base_hbm, wts_hbm, slp_hbm,
    ct_hbm, w_hbm, tw_hbm, fm_hbm,
    e_out, f_out,
    pos_ref, feat_ref, cnt_ref, rw_ref, mix_ref, ow_ref, cw_ref, base_ref, wts_ref, slp_ref,
    ct, w, tw, fm,
    halo, hpos, posb, pv, wk, dk, uu_, radt, msg, gm, gp_a, gp_b, own_acc, ff, fr,
    ee, wzx, spec, plane, back, field, grn,
    in_sem, hs, hr, ps, pr_, fs, fr_sem, as_, ar, bs, br, ls, phase,
):
    N = G * S
    MY = N
    g = lax.axis_index("gz")
    s = lax.axis_index("xy")
    me = g * S + s

    def peer(dz, dx):
        return (lax.rem(g + (dz + G), G), lax.rem(s + (dx + S), S))

    loads = [pltpu.make_async_copy(h, v, in_sem.at[i]) for i, (h, v) in enumerate([
        (feat_hbm, feat_ref), (cnt_hbm, cnt_ref), (cw_hbm, cw_ref), (base_hbm, base_ref),
        (wts_hbm, wts_ref), (slp_hbm, slp_ref), (pos_hbm, pos_ref), (ct_hbm, ct),
        (rw_hbm, rw_ref), (mix_hbm, mix_ref), (ow_hbm, ow_ref),
        (w_hbm, w), (tw_hbm, tw), (fm_hbm, fm)])]
    for t in loads:
        t.start()

    bar = pltpu.get_barrier_semaphore()
    diag = [(dz, dx) for dz in (-1, 1) for dx in (-1, 1)]
    for dz, dx in diag:
        pl.semaphore_signal(bar, inc=1, device_id=peer(dz, dx), device_id_type=MESH)
    for dz in range(1, G):
        pl.semaphore_signal(bar, inc=1, device_id=peer(dz, 0), device_id_type=MESH)

    def sig_row(k, _):
        pl.semaphore_signal(bar, inc=1, device_id=(g, lax.rem(s + k, S)), device_id_type=MESH)
        return 0

    lax.fori_loop(1, S, sig_row, 0)

    for t in loads[:8]:
        t.wait()
    lane = lax.broadcasted_iota(jnp.int32, (1, T), 1)
    valid = (lane < cnt_ref[...]).astype(F32)
    featv = feat_ref[...].astype(F32) * valid
    halo[4] = jnp.transpose(featv)
    hpos[4] = jnp.concatenate([pos_ref[c] for c in range(3)] + [jnp.zeros((5, T), F32)], axis=0)
    cwt = jnp.transpose(jnp.broadcast_to(cw_ref[...], (8, F)))
    charge = jnp.sum(featv * cwt[:, 0:1], axis=0, keepdims=True)

    yrow = lax.broadcasted_iota(jnp.int32, (MY, T), 0)
    ty = jnp.bitwise_and(yrow - base_ref[2] + 1, MY - 1)
    wy = jnp.zeros((MY, T), F32)
    sy = jnp.zeros((MY, T), F32)
    for c in range(4):
        hit = ty == c
        wy = wy + jnp.where(hit, wts_ref[8 + c], 0.0)
        sy = sy + jnp.where(hit, slp_ref[8 + c], 0.0)
    ab = lax.broadcasted_iota(jnp.int32, (ABP, T), 0)
    arow = lax.shift_right_logical(ab * 373, 12)
    brow = ab - arow * EX
    tz = arow - (base_ref[0] - g * BZ)
    tx = brow - (base_ref[1] - s * BX)
    zero = jnp.zeros((ABP, T), F32)
    wz, sz, wx, sx = zero, zero, zero, zero
    for c in range(4):
        hit = tz == c
        wz = wz + jnp.where(hit, wts_ref[c], 0.0)
        sz = sz + jnp.where(hit, slp_ref[c], 0.0)
        hit = tx == c
        wx = wx + jnp.where(hit, wts_ref[4 + c], 0.0)
        sx = sx + jnp.where(hit, slp_ref[4 + c], 0.0)
    wzx[0] = wz * wx
    wzx[1] = sz * wx
    wzx[2] = wz * sx

    yw = split(jnp.concatenate([wy, sy], axis=1))
    e_all = dot3((ct[0], ct[1]), yw, NN)
    eh, el = split(e_all)
    ee[0] = eh
    ee[1] = el
    spectrum = dot3((eh[:, :T], el[:, :T]), split(wzx[0] * charge), NT)
    spec[:, 0, :] = spectrum[:, :128]
    spec[:, 1, :] = spectrum[:, 128:]

    kk = lax.broadcasted_iota(jnp.int32, (N, 128), 0)
    hh = lax.broadcasted_iota(jnp.int32, (N, 128), 1)
    kz = kk // S + G * (hh // BX)
    kx = lax.rem(kk, S) + S * lax.rem(hh, BX)
    mz_, mx_ = G * BZ, S * BX
    kz = (kz - mz_ * (2 * kz >= mz_).astype(jnp.int32)).astype(F32)
    kx = (kx - mx_ * (2 * kx >= mx_).astype(jnp.int32)).astype(F32)
    ky = jnp.where(me <= MY // 2, me, me - MY // 2).astype(F32)
    twice = jnp.where(jnp.logical_or(me == 0, me == MY // 2), 1.0, 2.0)
    len_z, len_x = EDGE_LEN * G, EDGE_LEN * S
    fz, fx, fy = kz * (1.0 / len_z), kx * (1.0 / len_x), ky * (1.0 / PERIOD_Y)
    wsq = fz * fz + fx * fx + fy * fy
    positive = wsq > 0
    safe = jnp.where(positive, wsq, 1.0)
    green = COULOMB * jnp.exp(safe * (-np.pi ** 2 / EWALD_BETA ** 2)) / (
        np.pi * len_z * len_x * PERIOD_Y * safe)
    grn[...] = jnp.where(positive, green * twice, 0.0)

    own_t = jnp.transpose(hpos[4])
    for c in range(3):
        posb[c] = jnp.broadcast_to(own_t[:, c:c + 1], (T, T))

    lane_c = lax.broadcasted_iota(jnp.int32, (IC, T), 1)
    row_c = lax.broadcasted_iota(jnp.int32, (IC, T), 0)

    def pairs(n):
        off_z = (n // 3 - 1) * 1.0
        off_x = (lax.rem(n, 3) - 1) * 1.0
        near = [hpos[n, c:c + 1, :] for c in range(3)]

        def chunk(t, _):
            i0 = pl.multiple_of(t * IC, IC)
            rows = pl.ds(i0, IC)
            own = [posb[c, rows, :] for c in range(3)]
            same = jnp.logical_and(row_c + i0 == lane_c, n == 4)
            rinv, s1, c1, m, env, u = geometry(own, near, off_z, off_x, jnp.where(same, 0.0, 1.0))
            amp = env * rinv
            damp = -(m * (1.0 / 9.0) + env * (rinv * rinv))
            amp_r = amp * rinv
            amp_c = amp * (np.pi / CUTOFF)
            for c in range(3):
                uu_[n, c, rows, :] = u[c]
            two_c = 2.0 * c1
            s_prev, s_now = jnp.zeros_like(s1), s1
            c_prev, c_now = jnp.ones_like(c1), c1
            for k in range(K):
                lanes = slice(k * T, (k + 1) * T)
                e = s_now * amp
                pv[n, rows, lanes] = e.astype(BF16)
                for c in range(3):
                    pv[n, pl.ds((c + 1) * T + i0, IC), lanes] = (e * u[c]).astype(BF16)
                wk[n, k, rows, :] = s_now * amp_r
                dk[n, k, rows, :] = (c_now * float(k + 1)) * amp_c + s_now * damp
                s_prev, s_now = s_now, two_c * s_now - s_prev
                c_prev, c_now = c_now, two_c * c_now - c_prev
            return 0

        lax.fori_loop(0, T // IC, chunk, 0)

    pairs(jnp.int32(4))

    pl.semaphore_wait(bar, 4 + G - 1 + S - 1)

    def neighbour_copies(src, dst, send_sem, recv_sem, same_src):
        out = []
        for n, (dz, dx) in enumerate(OFFSETS):
            if n != 4:
                out.append(pltpu.make_async_remote_copy(
                    src_ref=src.at[4 if same_src else n], dst_ref=dst.at[8 - n],
                    send_sem=send_sem.at[n], recv_sem=recv_sem.at[8 - n],
                    device_id=peer(dz, dx), device_id_type=MESH))
        return out

    pos_copies = neighbour_copies(hpos, hpos, ps, pr_, True)
    for cp in pos_copies:
        cp.start()

    def sig_phase(k, _):
        pl.semaphore_signal(phase, inc=1, device_id=(g, lax.rem(s + k, S)), device_id_type=MESH)
        return 0

    lax.fori_loop(1, S, sig_phase, 0)
    pl.semaphore_wait(phase, S - 1)

    def exchange(src, dst, send_sem, recv_sem):
        own = pltpu.make_async_copy(src.at[me], dst.at[me], ls)
        own.start()

        def send(k, _):
            q = lax.rem(me + k, N)
            pltpu.make_async_remote_copy(
                src_ref=src.at[q], dst_ref=dst.at[me], send_sem=send_sem, recv_sem=recv_sem,
                device_id=(q // S, lax.rem(q, S)), device_id_type=MESH).start()
            return 0

        lax.fori_loop(1, N, send, 0)
        own.wait()

    def arrived(dst, sem):
        pltpu.make_async_copy(dst.at[pl.ds(0, N - 1)], dst.at[pl.ds(0, N - 1)], sem).wait()

    exchange(spec, plane, as_, ar)
    halo_copies = neighbour_copies(halo, halo, hs, hr, True)
    for cp in halo_copies:
        cp.start()

    for cp in pos_copies:
        cp.wait_recv()

    def pair_step(q, _):
        pairs(q + (q >= 4).astype(jnp.int32))
        return 0

    lax.fori_loop(0, 8, pair_step, 0)

    for t in loads[8:]:
        t.wait()
    arrived(plane, ar)
    rs = split(jnp.concatenate([plane[:, 0, :], plane[:, 1, :]], axis=1))
    yr = dot3((w[0, 0:N], w[1, 0:N]), rs, NN)
    yi = dot3((w[0, N:], w[1, N:]), rs, NN)
    tr, ti = tw[0], tw[1]
    yy = split(jnp.concatenate([tr * yr - ti * yi, tr * yi + ti * yr], axis=1))
    zz = dot3(yy, (fm[0], fm[1]), NN)
    zs = split(zz * jnp.concatenate([grn[...], grn[...]], axis=1))
    vv = dot3(zs, (fm[0], fm[1]), NT)
    vr, vi = vv[:, :ABP], vv[:, ABP:]
    p_r = split(tr * vr + ti * vi)
    p_i = split(tr * vi - ti * vr)
    uu = dot3((w[0, 0:N], w[1, 0:N]), p_r, NN) + dot3((w[0, N:], w[1, N:]), p_i, NN)
    back[:, 0, :] = uu[:, :128]
    back[:, 1, :] = uu[:, 128:]
    exchange(back, field, bs, br)

    for cp in halo_copies:
        cp.wait_recv()
    msg[...] = jnp.zeros_like(msg)

    def forward(n, _):
        feat = halo[n]
        for k in range(K):
            radt[n, k * T:(k + 1) * T, :] = (feat * rw_ref[k:k + 1, :]).astype(BF16)
        msg[...] += dg(pv[n], radt[n], NN)
        return 0

    lax.fori_loop(0, 9, forward, 0)

    m0 = msg[0:T]
    mc = [msg[(c + 1) * T:(c + 2) * T] for c in range(3)]
    inv = (m0 + (mc[0] * mc[0] + mc[1] * mc[1] + mc[2] * mc[2])).astype(BF16)
    mix = mix_ref[...]
    pre = dg(inv, mix, NN)
    sig = 1.0 / (1.0 + jnp.exp(-pre))
    owr = ow_ref[...]
    energy_col = jnp.sum(pre * sig * owr, axis=1, keepdims=True)
    energy_sr = jnp.transpose(jnp.broadcast_to(energy_col, (T, T)))[0:1, :]
    valid_col = jnp.transpose(jnp.broadcast_to(valid, (8, T)))[:, 0:1]
    grad_pre = ((sig + pre * sig * (1.0 - sig)) * owr * valid_col).astype(BF16)
    grad_inv = dg(grad_pre, mix, NT)
    gm[0:T] = grad_inv.astype(BF16)
    for c in range(3):
        gm[(c + 1) * T:(c + 2) * T] = (2.0 * mc[c] * grad_inv).astype(BF16)

    own_acc[...] = jnp.zeros_like(own_acc)

    def grad_dot(n, gp):
        gp[...] = dg(gm[...], radt[n], NT)

    def grad_pairs(n, gp):
        near = [None] * 3
        for t in range(T // 8):
            rows = slice(t * 8, (t + 1) * 8)
            tc = [None] * 3
            bb = [None] * 4
            for k in range(K):
                lanes = slice(k * T, (k + 1) * T)
                wv, dv = wk[n, k, rows, :], dk[n, k, rows, :]
                for c in range(4):
                    v = gp[c * T + t * 8:c * T + (t + 1) * 8, lanes]
                    bb[c] = v * dv if k == 0 else bb[c] + v * dv
                    if c:
                        tc[c - 1] = v * wv if k == 0 else tc[c - 1] + v * wv
            u = [uu_[n, c, rows, :] for c in range(3)]
            b = bb[0]
            for c in range(3):
                b = b + u[c] * (bb[c + 1] - tc[c])
            for c in range(3):
                gr = tc[c] + u[c] * b
                own_acc[c, rows, :] += gr
                near[c] = gr if t == 0 else near[c] + gr
        for c in range(3):
            ff[n, c:c + 1, :] = -jnp.sum(near[c], axis=0, keepdims=True)

    ff[...] = jnp.zeros_like(ff)
    grad_dot(0, gp_a)

    def backward(t, _):
        grad_dot(2 * t + 1, gp_b)
        grad_pairs(2 * t, gp_a)
        grad_dot(2 * t + 2, gp_a)
        grad_pairs(2 * t + 1, gp_b)
        return 0

    lax.fori_loop(0, 4, backward, 0)
    grad_pairs(8, gp_a)

    force_copies = neighbour_copies(ff, fr, fs, fr_sem, False)
    for cp in force_copies:
        cp.start()

    arrived(field, br)
    phi = split(jnp.concatenate([field[:, 0, :], field[:, 1, :]], axis=1))
    along = dot3(phi, (ee[0], ee[1]), TN)
    a_w, a_s = along[:, :T], along[:, T:]
    pot = jnp.sum(a_w * wzx[0], axis=0, keepdims=True)
    rec = [
        -charge * jnp.sum(a_w * wzx[1], axis=0, keepdims=True),
        -charge * jnp.sum(a_w * wzx[2], axis=0, keepdims=True),
        -charge * jnp.sum(a_s * wzx[0], axis=0, keepdims=True),
    ]
    e_out[...] = valid * (energy_sr + 0.5 * charge * pot)
    own_rows = []
    for c in range(3):
        col = jnp.sum(own_acc[c], axis=1, keepdims=True)
        own_rows.append(jnp.transpose(jnp.broadcast_to(col, (T, T)))[0:1, :])

    for cp in force_copies:
        cp.wait_recv()
    near = ff[4]
    for n in range(9):
        if n != 4:
            near = near + fr[n]
    for c in range(3):
        f_out[c] = own_rows[c] + near[c:c + 1, :] + rec[c]
    for cp in pos_copies + halo_copies + force_copies:
        cp.wait_send()
    arrived(spec, as_)
    arrived(back, bs)


def local(G, S, positions, features, cell_counts, radial_weights, mix_weights, out_weights,
          charge_weights, spline_base, spline_weights, spline_slopes):
    N = G * S
    hbm = pl.BlockSpec(memory_space=pltpu.HBM)
    vm = pl.BlockSpec(memory_space=pltpu.VMEM)
    V = pltpu.VMEM
    DMA = pltpu.SemaphoreType.DMA
    e, f = pl.pallas_call(
        functools.partial(kernel, G, S),
        out_shape=(jax.ShapeDtypeStruct((1, T), F32), jax.ShapeDtypeStruct((3, 1, T), F32)),
        in_specs=[hbm] * 14,
        out_specs=[vm, vm],
        scratch_shapes=[
            V((3, 1, T), F32), V((F, T), BF16), V((1, 1), jnp.int32), V((K, F), F32), V((F, F), BF16),
            V((1, F), F32), V((1, F), F32), V((3, 1, T), jnp.int32), V((12, 1, T), F32), V((12, 1, T), F32),
            V((2, N, N), BF16), V((2, 2 * N, N), BF16), V((2, N, ABP), F32), V((2, 2 * ABP, 256), BF16),
            V((9, T, F), F32), V((9, 8, T), F32), V((3, T, T), F32), V((9, 4 * T, K * T), BF16),
            V((9, K, T, T), F32), V((9, K, T, T), F32), V((9, 3, T, T), F32), V((9, K * T, F), BF16),
            V((4 * T, F), F32), V((4 * T, F), BF16), V((4 * T, K * T), F32), V((4 * T, K * T), F32),
            V((3, T, T), F32), V((9, 8, T), F32), V((9, 8, T), F32),
            V((2, N, 2 * T), BF16), V((3, ABP, T), F32),
            V((N, 2, 128), F32), V((N, 2, 128), F32), V((N, 2, 128), F32), V((N, 2, 128), F32),
            V((N, 128), F32),
            DMA((14,)), DMA((9,)), DMA((9,)), DMA((9,)), DMA((9,)), DMA((9,)), DMA((9,)),
            DMA, DMA, DMA, DMA, DMA, pltpu.SemaphoreType.REGULAR,
        ],
        compiler_params=pltpu.CompilerParams(collective_id=0, has_side_effects=True,
                                             vmem_limit_bytes=60 * 1024 * 1024),
    )(
        positions.reshape(3, 1, T), features.reshape(F, T), cell_counts, radial_weights, mix_weights,
        out_weights.reshape(1, F), charge_weights.reshape(1, F), spline_base.reshape(3, 1, T),
        spline_weights.reshape(12, 1, T), spline_slopes.reshape(12, 1, T),
        *[jnp.asarray(t) for t in tables(G, S)],
    )
    return e.reshape(1, 1, T), f.reshape(3, 1, 1, T)


def solution(mesh):
    placed = (
        P(None, "gz", "xy", None), P(None, "gz", "xy", None), P("gz", "xy"), P(), P(), P(), P(),
        P(None, "gz", "xy", None), P(None, None, "gz", "xy", None), P(None, None, "gz", "xy", None),
    )
    return jax.shard_map(
        functools.partial(local, mesh.shape["gz"], mesh.shape["xy"]),
        mesh=mesh, in_specs=placed,
        out_specs=(P("gz", "xy", None), P(None, "gz", "xy", None)),
        check_vma=False,
    )
```

```python
import functools

import jax
import jax.numpy as jnp
import numpy as np
from jax import lax
from jax.experimental import pallas as pl
from jax.experimental.pallas import tpu as pltpu
from jax.sharding import PartitionSpec as P

MESH = pl.DeviceIdType.MESH
F32 = jnp.float32
BF16 = jnp.bfloat16

K = 8
F = 128
T = 128
BZ = 16
BX = 8
EZ = BZ + 3
EX = BX + 3
ABP = 256
EDGE_LEN = 6.0
PERIOD_Y = 36.0
CUTOFF = 6.0
SOFTEN = 0.04
EWALD_BETA = 8.0
COULOMB = 4.0
IC = 32
OFFSETS = [(dz, dx) for dz in (-1, 0, 1) for dx in (-1, 0, 1)]


def split_np(x):
    x = np.asarray(x, np.float32)
    hi = x.astype(jnp.bfloat16)
    lo = (x - hi.astype(np.float32)).astype(jnp.bfloat16)
    return np.stack([hi, lo])


def half_rows(N):
    return -(-(N // 2 + 2) // 16) * 16


@functools.lru_cache(None)
def tables(G, S):
    MZ, MX, MY, N = G * BZ, S * BX, G * S, G * S
    p = np.arange(MY)
    ky = np.where(p <= MY // 2, p, p - MY // 2)
    ang = 2 * np.pi * ((ky[:, None] * np.arange(MY)[None, :]) % MY) / MY
    ct = np.where((p <= MY // 2)[:, None], np.cos(ang), np.sin(ang))
    kzl = np.repeat(np.arange(G), S)
    kxl = np.tile(np.arange(S), G)
    mate = (-kzl % G) * S + (-kxl % S)
    rows = np.arange(N)
    kept = rows[rows <= mate]
    count = np.where(kept == mate[kept], 1.0, 2.0)
    fill = half_rows(N) - len(kept)
    kept = np.concatenate([kept, np.zeros(fill, np.int64)])
    count = np.concatenate([count, np.zeros(fill)])
    rz, rx = kzl[kept], kxl[kept]
    ang = 2 * np.pi * (((rz[:, None] * kzl[None, :]) % G) / G + ((rx[:, None] * kxl[None, :]) % S) / S)
    w = np.concatenate([np.cos(ang), -np.sin(ang)], axis=0)
    a = np.repeat(np.arange(EZ), EX)
    b = np.tile(np.arange(EX), EZ)
    ang = 2 * np.pi * (rz[:, None] * (a - 1)[None] / MZ + rx[:, None] * (b - 1)[None] / MX)
    pad = ((0, 0), (0, ABP - EZ * EX))
    tw = np.stack([np.pad(np.cos(ang), pad), np.pad(-np.sin(ang), pad)]).astype(np.float32)
    kzh = np.repeat(np.arange(BZ), BX)
    kxh = np.tile(np.arange(BX), BZ)
    ang = 2 * np.pi * ((a - 1)[:, None] * kzh[None] / BZ + (b - 1)[:, None] * kxh[None] / BX)
    pad = ((0, ABP - EZ * EX), (0, 0))
    mr, mi = np.pad(np.cos(ang), pad), np.pad(-np.sin(ang), pad)
    fm = np.block([[mr, mi], [-mi, mr]])
    kz = rz[:, None] + G * kzh[None]
    kx = rx[:, None] + S * kxh[None]
    kz = kz - MZ * (2 * kz >= MZ)
    kx = kx - MX * (2 * kx >= MX)
    wave = (kz / (EDGE_LEN * G)) ** 2 + (kx / (EDGE_LEN * S)) ** 2
    scale = np.broadcast_to(count[:, None], wave.shape)
    gr = np.stack([wave, scale]).astype(np.float32)
    return split_np(ct), split_np(w), split_np(w.T), tw, split_np(fm), gr


def fit(fn, degree, top):
    z = top * (0.5 - 0.5 * np.cos(np.pi * (np.arange(200) + 0.5) / 200))
    return [float(c) for c in np.polynomial.polynomial.polyfit(z, fn(z), degree)]


COS_C = fit(lambda z: np.cos(np.pi * np.sqrt(z)), 6, 0.2526)
SIN_C = fit(lambda z: np.sin(np.pi * np.sqrt(z + 1e-300)) / np.sqrt(z + 1e-300), 5, 0.2526)


def poly(coefs, z):
    acc = jnp.full_like(z, coefs[-1])
    for c in coefs[-2::-1]:
        acc = acc * z + c
    return acc


def split(x):
    hi = x.astype(BF16)
    return hi, (x - hi.astype(F32)).astype(BF16)


def dg(a, b, dims):
    return lax.dot_general(a, b, (dims, ((), ())), preferred_element_type=F32)


NN = ((1,), (0,))
NT = ((1,), (1,))
TN = ((0,), (0,))


def dot3(a, b, dims):
    return dg(a[0], b[0], dims) + (dg(a[0], b[1], dims) + dg(a[1], b[0], dims))


def geometry(own, near, off_z, off_x, keep):
    dz = (off_z + near[0] - own[0]) * EDGE_LEN
    dx = (off_x + near[1] - own[1]) * EDGE_LEN
    dy = near[2] - own[2]
    dy = jnp.where(dy > 0.5, dy - 1.0, jnp.where(dy < -0.5, dy + 1.0, dy)) * PERIOD_Y
    rsq = dz * dz + dx * dx + dy * dy
    r2 = rsq + SOFTEN
    rinv = lax.rsqrt(r2)
    r = r2 * rinv
    x = jnp.minimum(r, 6.014) * (1.0 / CUTOFF) - 0.5
    z = x * x
    s1 = poly(COS_C, z)
    c1 = -x * poly(SIN_C, z)
    m = jnp.maximum(1.0 - rsq * (1.0 / (CUTOFF * CUTOFF)), 0.0) * keep
    env = m * m
    u = (dz * rinv, dx * rinv, dy * rinv)
    return rinv, s1, c1, m, env, u


def kernel(
    G, S,
    pos_hbm, feat_hbm, cnt_hbm, rw_hbm, mix_hbm, ow_hbm, cw_hbm, base_hbm, wts_hbm, slp_hbm,
    ct_hbm, w_hbm, wt_hbm, tw_hbm, fm_hbm, gr_hbm,
    e_out, f_out,
    pos_ref, feat_ref, cnt_ref, rw_ref, mix_ref, ow_ref, cw_ref, base_ref, wts_ref, slp_ref,
    ct, w, wt, tw, fm, gr,
    halo, hpos, posb, pv, wk, dk, uu_, radt, msg, gm, gp_a, gp_b, own_acc, ff, fr,
    ee, wzx, spec, plane, back, field, grn,
    in_sem, hs, hr, ps, pr_, fs, fr_sem, as_, ar, bs, br, ls, phase,
):
    N = G * S
    MY = N
    g = lax.axis_index("gz")
    s = lax.axis_index("xy")
    me = g * S + s

    def peer(dz, dx):
        return (lax.rem(g + (dz + G), G), lax.rem(s + (dx + S), S))

    loads = [pltpu.make_async_copy(h, v, in_sem.at[i]) for i, (h, v) in enumerate([
        (feat_hbm, feat_ref), (cnt_hbm, cnt_ref), (cw_hbm, cw_ref), (base_hbm, base_ref),
        (wts_hbm, wts_ref), (slp_hbm, slp_ref), (pos_hbm, pos_ref), (ct_hbm, ct),
        (rw_hbm, rw_ref), (mix_hbm, mix_ref), (ow_hbm, ow_ref),
        (w_hbm, w), (wt_hbm, wt), (tw_hbm, tw), (fm_hbm, fm), (gr_hbm, gr)])]
    for t in loads:
        t.start()

    bar = pltpu.get_barrier_semaphore()
    diag = [(dz, dx) for dz in (-1, 1) for dx in (-1, 1)]
    for dz, dx in diag:
        pl.semaphore_signal(bar, inc=1, device_id=peer(dz, dx), device_id_type=MESH)
    for dz in range(1, G):
        pl.semaphore_signal(bar, inc=1, device_id=peer(dz, 0), device_id_type=MESH)

    def sig_row(k, _):
        pl.semaphore_signal(bar, inc=1, device_id=(g, lax.rem(s + k, S)), device_id_type=MESH)
        return 0

    lax.fori_loop(1, S, sig_row, 0)

    for t in loads[:8]:
        t.wait()
    lane = lax.broadcasted_iota(jnp.int32, (1, T), 1)
    valid = (lane < cnt_ref[...]).astype(F32)
    featv = feat_ref[...].astype(F32) * valid
    halo[4] = jnp.transpose(featv)
    hpos[4] = jnp.concatenate([pos_ref[c] for c in range(3)] + [jnp.zeros((5, T), F32)], axis=0)
    cwt = jnp.transpose(jnp.broadcast_to(cw_ref[...], (8, F)))
    charge = jnp.sum(featv * cwt[:, 0:1], axis=0, keepdims=True)

    yrow = lax.broadcasted_iota(jnp.int32, (MY, T), 0)
    ty = jnp.bitwise_and(yrow - base_ref[2] + 1, MY - 1)
    wy = jnp.zeros((MY, T), F32)
    for c in range(4):
        wy = wy + jnp.where(ty == c, wts_ref[8 + c], 0.0)
    ab = lax.broadcasted_iota(jnp.int32, (ABP, T), 0)
    arow = lax.shift_right_logical(ab * 373, 12)
    brow = ab - arow * EX
    tz = arow - (base_ref[0] - g * BZ)
    tx = brow - (base_ref[1] - s * BX)
    zero = jnp.zeros((ABP, T), F32)
    wz, wx = zero, zero
    for c in range(4):
        wz = wz + jnp.where(tz == c, wts_ref[c], 0.0)
        wx = wx + jnp.where(tx == c, wts_ref[4 + c], 0.0)
    wzx[0] = wz * wx

    eh, el = split(dot3((ct[0], ct[1]), split(wy), NN))
    ee[0, :, :T] = eh
    ee[1, :, :T] = el
    spectrum = dot3((eh, el), split(wz * wx * charge), NT)
    spec[:, 0, :] = spectrum[:, :128]
    spec[:, 1, :] = spectrum[:, 128:]

    pl.semaphore_wait(bar, 4 + G - 1 + S - 1)

    def neighbour_copies(src, dst, send_sem, recv_sem, same_src):
        out = []
        for n, (dz, dx) in enumerate(OFFSETS):
            if n != 4:
                out.append(pltpu.make_async_remote_copy(
                    src_ref=src.at[4 if same_src else n], dst_ref=dst.at[8 - n],
                    send_sem=send_sem.at[n], recv_sem=recv_sem.at[8 - n],
                    device_id=peer(dz, dx), device_id_type=MESH))
        return out

    pos_copies = neighbour_copies(hpos, hpos, ps, pr_, True)
    for cp in pos_copies:
        cp.start()

    def feature_copy(src, dst, dz, dx):
        return pltpu.make_async_remote_copy(
            src_ref=halo.at[src], dst_ref=halo.at[dst], send_sem=hs.at[dst], recv_sem=hr.at[dst],
            device_id=peer(dz, dx), device_id_type=MESH)

    side_z = [feature_copy(4, 1, 1, 0), feature_copy(4, 7, -1, 0)]
    side_x = [feature_copy(4, 3, 0, 1), feature_copy(4, 5, 0, -1)]
    corners = [feature_copy(1, 0, 0, 1), feature_copy(1, 2, 0, -1),
               feature_copy(7, 6, 0, 1), feature_copy(7, 8, 0, -1)]
    for cp in side_z + side_x:
        cp.start()

    def sig_phase(k, _):
        pl.semaphore_signal(phase, inc=1, device_id=(g, lax.rem(s + k, S)), device_id_type=MESH)
        return 0

    lax.fori_loop(1, S, sig_phase, 0)
    own_t = jnp.transpose(hpos[4])
    for c in range(3):
        posb[c] = jnp.broadcast_to(own_t[:, c:c + 1], (T, T))

    lane_c = lax.broadcasted_iota(jnp.int32, (IC, T), 1)
    row_c = lax.broadcasted_iota(jnp.int32, (IC, T), 0)

    def pairs(n):
        off_z = (n // 3 - 1) * 1.0
        off_x = (lax.rem(n, 3) - 1) * 1.0
        near = [hpos[n, c:c + 1, :] for c in range(3)]

        def chunk(t, _):
            i0 = pl.multiple_of(t * IC, IC)
            rows = pl.ds(i0, IC)
            own = [posb[c, rows, :] for c in range(3)]
            same = jnp.logical_and(row_c + i0 == lane_c, n == 4)
            rinv, s1, c1, m, env, u = geometry(own, near, off_z, off_x, jnp.where(same, 0.0, 1.0))
            amp = env * rinv
            damp = -(m * (1.0 / 9.0) + env * (rinv * rinv))
            amp_r = amp * rinv
            amp_c = amp * (np.pi / CUTOFF)
            for c in range(3):
                uu_[n, c, rows, :] = u[c]
            two_c = 2.0 * c1
            s_prev, s_now = jnp.zeros_like(s1), s1
            c_prev, c_now = jnp.ones_like(c1), c1
            for k in range(K):
                lanes = slice(k * T, (k + 1) * T)
                e = s_now * amp
                pv[n, rows, lanes] = e.astype(BF16)
                for c in range(3):
                    pv[n, pl.ds((c + 1) * T + i0, IC), lanes] = (e * u[c]).astype(BF16)
                wk[n, k, rows, :] = s_now * amp_r
                dk[n, k, rows, :] = (c_now * float(k + 1)) * amp_c + s_now * damp
                s_prev, s_now = s_now, two_c * s_now - s_prev
                c_prev, c_now = c_now, two_c * c_now - c_prev
            return 0

        lax.fori_loop(0, T // IC, chunk, 0)

    pairs(jnp.int32(4))

    pl.semaphore_wait(phase, S - 1)

    def exchange(src, dst, send_sem, recv_sem):
        own = pltpu.make_async_copy(src.at[me], dst.at[me], ls)
        own.start()

        def one(j, dz):
            x2 = lax.bitwise_and((g // 2) + lax.bitwise_and(lax.shift_right_logical(0x36, 2 * (j // 8)), 3), 3)
            dy = lax.bitwise_and(lax.shift_right_logical(0x36, 2 * lax.rem(j // 2, 4)), 3)
            y2 = lax.bitwise_and(2 * lax.rem(g, 2) + lax.rem(s // 2, 2) + dy, 3)
            z2 = lax.bitwise_and(s // 4 + dz, 7)
            gq = 2 * x2 + y2 // 2
            sq = 4 * z2 + 2 * lax.rem(y2, 2) + lax.rem(s + j + 1, 2)
            pltpu.make_async_remote_copy(
                src_ref=src.at[gq * S + sq], dst_ref=dst.at[me], send_sem=send_sem, recv_sem=recv_sem,
                device_id=(gq, sq), device_id_type=MESH).start()

        def send(j, _):
            for dz in (4, 5, 3, 6, 2, 7, 1, 0):
                one(j, dz)
            return 0

        lax.fori_loop(0, 31, send, 0)
        for dz in (4, 5, 3, 6, 2, 7, 1):
            one(jnp.int32(31), dz)
        own.wait()

    def arrived(dst, sem):
        pltpu.make_async_copy(dst.at[pl.ds(0, N - 1)], dst.at[pl.ds(0, N - 1)], sem).wait()

    exchange(spec, plane, as_, ar)

    sy = jnp.zeros((MY, T), F32)
    for c in range(4):
        sy = sy + jnp.where(ty == c, slp_ref[8 + c], 0.0)
    eh, el = split(dot3((ct[0], ct[1]), split(sy), NN))
    ee[0, :, T:] = eh
    ee[1, :, T:] = el
    wz, sz, wx, sx = zero, zero, zero, zero
    for c in range(4):
        hit = tz == c
        wz = wz + jnp.where(hit, wts_ref[c], 0.0)
        sz = sz + jnp.where(hit, slp_ref[c], 0.0)
        hit = tx == c
        wx = wx + jnp.where(hit, wts_ref[4 + c], 0.0)
        sx = sx + jnp.where(hit, slp_ref[4 + c], 0.0)
    wzx[1] = sz * wx
    wzx[2] = wz * sx
    for t in loads[8:]:
        t.wait()
    ky = jnp.where(me <= MY // 2, me, me - MY // 2).astype(F32) * (1.0 / PERIOD_Y)
    twice = jnp.where(jnp.logical_or(me == 0, me == MY // 2), 1.0, 2.0)
    wsq = gr[0] + ky * ky
    positive = wsq > 0
    safe = jnp.where(positive, wsq, 1.0)
    green = COULOMB * jnp.exp(safe * (-np.pi ** 2 / EWALD_BETA ** 2)) / (
        (np.pi * EDGE_LEN * G * EDGE_LEN * S * PERIOD_Y) * safe)
    grn[...] = jnp.where(positive, green * twice, 0.0) * gr[1]

    for cp in pos_copies:
        cp.wait_recv()

    def pair_step(q, _):
        pairs(q + (q >= 4).astype(jnp.int32))
        return 0

    lax.fori_loop(0, 4, pair_step, 0)
    for cp in side_z:
        cp.wait_recv()
    for cp in corners:
        cp.start()
    lax.fori_loop(4, 8, pair_step, 0)

    msg[...] = jnp.zeros_like(msg)

    def forward(n):
        feat = halo[n]
        for k in range(K):
            radt[n, k * T:(k + 1) * T, :] = (feat * rw_ref[k:k + 1, :]).astype(BF16)
        msg[...] += dg(pv[n], radt[n], NN)
        return 0

    for cp in side_x:
        cp.wait_recv()
    forward(4)
    lax.fori_loop(0, 4, lambda q, _: forward(2 * q + 1), 0)

    arrived(plane, ar)
    rs = split(jnp.concatenate([plane[:, 0, :], plane[:, 1, :]], axis=1))
    y_all = dot3((w[0], w[1]), rs, NN)
    H = half_rows(N)
    yr, yi = y_all[:H], y_all[H:]
    tr, ti = tw[0], tw[1]
    yy = split(jnp.concatenate([tr * yr - ti * yi, tr * yi + ti * yr], axis=1))
    zz = dot3(yy, (fm[0], fm[1]), NN)
    zs = split(zz * jnp.concatenate([grn[...], grn[...]], axis=1))
    vv = dot3(zs, (fm[0], fm[1]), NT)
    vr, vi = vv[:, :ABP], vv[:, ABP:]
    vs = split(jnp.concatenate([tr * vr + ti * vi, tr * vi - ti * vr], axis=0))
    uu = dot3((wt[0], wt[1]), vs, NN)
    back[:, 0, :] = uu[:, :128]
    back[:, 1, :] = uu[:, 128:]
    exchange(back, field, bs, br)

    for cp in corners:
        cp.wait_recv()
    lax.fori_loop(0, 4, lambda q, _: forward(2 * q + 2 * (q >= 2).astype(jnp.int32)), 0)

    m0 = msg[0:T]
    mc = [msg[(c + 1) * T:(c + 2) * T] for c in range(3)]
    inv = (m0 + (mc[0] * mc[0] + mc[1] * mc[1] + mc[2] * mc[2])).astype(BF16)
    mix = mix_ref[...]
    pre = dg(inv, mix, NN)
    sig = 1.0 / (1.0 + jnp.exp(-pre))
    owr = ow_ref[...]
    energy_col = jnp.sum(pre * sig * owr, axis=1, keepdims=True)
    energy_sr = jnp.transpose(jnp.broadcast_to(energy_col, (T, T)))[0:1, :]
    valid_col = jnp.transpose(jnp.broadcast_to(valid, (8, T)))[:, 0:1]
    grad_pre = ((sig + pre * sig * (1.0 - sig)) * owr * valid_col).astype(BF16)
    grad_inv = dg(grad_pre, mix, NT)
    gm[0:T] = grad_inv.astype(BF16)
    for c in range(3):
        gm[(c + 1) * T:(c + 2) * T] = (2.0 * mc[c] * grad_inv).astype(BF16)

    own_acc[...] = jnp.zeros_like(own_acc)

    def grad_dot(n, gp):
        gp[...] = dg(gm[...], radt[n], NT)

    def grad_pairs(n, gp):
        near = [None] * 3
        for t in range(T // 8):
            rows = slice(t * 8, (t + 1) * 8)
            tc = [None] * 3
            bb = [None] * 4
            for k in range(K):
                lanes = slice(k * T, (k + 1) * T)
                wv, dv = wk[n, k, rows, :], dk[n, k, rows, :]
                for c in range(4):
                    v = gp[c * T + t * 8:c * T + (t + 1) * 8, lanes]
                    bb[c] = v * dv if k == 0 else bb[c] + v * dv
                    if c:
                        tc[c - 1] = v * wv if k == 0 else tc[c - 1] + v * wv
            u = [uu_[n, c, rows, :] for c in range(3)]
            b = bb[0]
            for c in range(3):
                b = b + u[c] * (bb[c + 1] - tc[c])
            for c in range(3):
                gr = tc[c] + u[c] * b
                own_acc[c, rows, :] += gr
                near[c] = gr if t == 0 else near[c] + gr
        for c in range(3):
            ff[n, c:c + 1, :] = -jnp.sum(near[c], axis=0, keepdims=True)

    ff[...] = jnp.zeros_like(ff)
    grad_dot(0, gp_a)

    def backward(t, _):
        grad_dot(2 * t + 1, gp_b)
        grad_pairs(2 * t, gp_a)
        grad_dot(2 * t + 2, gp_a)
        grad_pairs(2 * t + 1, gp_b)
        return 0

    lax.fori_loop(0, 4, backward, 0)
    grad_pairs(8, gp_a)

    force_copies = neighbour_copies(ff, fr, fs, fr_sem, False)
    for cp in force_copies:
        cp.start()

    arrived(field, br)
    phi = split(jnp.concatenate([field[:, 0, :], field[:, 1, :]], axis=1))
    along = dot3(phi, (ee[0], ee[1]), TN)
    a_w, a_s = along[:, :T], along[:, T:]
    pot = jnp.sum(a_w * wzx[0], axis=0, keepdims=True)
    rec = [
        -charge * jnp.sum(a_w * wzx[1], axis=0, keepdims=True),
        -charge * jnp.sum(a_w * wzx[2], axis=0, keepdims=True),
        -charge * jnp.sum(a_s * wzx[0], axis=0, keepdims=True),
    ]
    e_out[...] = valid * (energy_sr + 0.5 * charge * pot)
    own_rows = []
    for c in range(3):
        col = jnp.sum(own_acc[c], axis=1, keepdims=True)
        own_rows.append(jnp.transpose(jnp.broadcast_to(col, (T, T)))[0:1, :])

    for cp in force_copies:
        cp.wait_recv()
    near = ff[4]
    for n in range(9):
        if n != 4:
            near = near + fr[n]
    for c in range(3):
        f_out[c] = own_rows[c] + near[c:c + 1, :] + rec[c]
    for cp in pos_copies + side_z + side_x + corners + force_copies:
        cp.wait_send()
    arrived(spec, as_)
    arrived(back, bs)


def local(G, S, positions, features, cell_counts, radial_weights, mix_weights, out_weights,
          charge_weights, spline_base, spline_weights, spline_slopes):
    N = G * S
    H = half_rows(N)
    hbm = pl.BlockSpec(memory_space=pltpu.HBM)
    vm = pl.BlockSpec(memory_space=pltpu.VMEM)
    V = pltpu.VMEM
    DMA = pltpu.SemaphoreType.DMA
    e, f = pl.pallas_call(
        functools.partial(kernel, G, S),
        out_shape=(jax.ShapeDtypeStruct((1, T), F32), jax.ShapeDtypeStruct((3, 1, T), F32)),
        in_specs=[hbm] * 16,
        out_specs=[vm, vm],
        scratch_shapes=[
            V((3, 1, T), F32), V((F, T), BF16), V((1, 1), jnp.int32), V((K, F), F32), V((F, F), BF16),
            V((1, F), F32), V((1, F), F32), V((3, 1, T), jnp.int32), V((12, 1, T), F32), V((12, 1, T), F32),
            V((2, N, N), BF16), V((2, 2 * H, N), BF16), V((2, N, 2 * H), BF16), V((2, H, ABP), F32), V((2, 2 * ABP, 256), BF16),
            V((2, H, 128), F32),
            V((9, T, F), F32), V((9, 8, T), F32), V((3, T, T), F32), V((9, 4 * T, K * T), BF16),
            V((9, K, T, T), F32), V((9, K, T, T), F32), V((9, 3, T, T), F32), V((9, K * T, F), BF16),
            V((4 * T, F), F32), V((4 * T, F), BF16), V((4 * T, K * T), F32), V((4 * T, K * T), F32),
            V((3, T, T), F32), V((9, 8, T), F32), V((9, 8, T), F32),
            V((2, N, 2 * T), BF16), V((3, ABP, T), F32),
            V((N, 2, 128), F32), V((N, 2, 128), F32), V((N, 2, 128), F32), V((N, 2, 128), F32),
            V((H, 128), F32),
            DMA((16,)), DMA((9,)), DMA((9,)), DMA((9,)), DMA((9,)), DMA((9,)), DMA((9,)),
            DMA, DMA, DMA, DMA, DMA, pltpu.SemaphoreType.REGULAR,
        ],
        compiler_params=pltpu.CompilerParams(collective_id=0, has_side_effects=True,
                                             vmem_limit_bytes=60 * 1024 * 1024),
    )(
        positions.reshape(3, 1, T), features.reshape(F, T), cell_counts, radial_weights, mix_weights,
        out_weights.reshape(1, F), charge_weights.reshape(1, F), spline_base.reshape(3, 1, T),
        spline_weights.reshape(12, 1, T), spline_slopes.reshape(12, 1, T),
        *[jnp.asarray(t) for t in tables(G, S)],
    )
    return e.reshape(1, 1, T), f.reshape(3, 1, 1, T)


def solution(mesh):
    placed = (
        P(None, "gz", "xy", None), P(None, "gz", "xy", None), P("gz", "xy"), P(), P(), P(), P(),
        P(None, "gz", "xy", None), P(None, None, "gz", "xy", None), P(None, None, "gz", "xy", None),
    )
    return jax.shard_map(
        functools.partial(local, mesh.shape["gz"], mesh.shape["xy"]),
        mesh=mesh, in_specs=placed,
        out_specs=(P("gz", "xy", None), P(None, "gz", "xy", None)),
        check_vma=False,
    )
```

```python
import functools

import jax
import jax.numpy as jnp
import numpy as np
from jax import lax
from jax.experimental import pallas as pl
from jax.experimental.pallas import tpu as pltpu
from jax.sharding import PartitionSpec as P

MESH = pl.DeviceIdType.MESH
F32 = jnp.float32
BF16 = jnp.bfloat16

K = 8
F = 128
T = 128
BZ = 16
BX = 8
EZ = BZ + 3
EX = BX + 3
ABP = 256
EDGE_LEN = 6.0
PERIOD_Y = 36.0
CUTOFF = 6.0
SOFTEN = 0.04
EWALD_BETA = 8.0
COULOMB = 4.0
IC = 32
OFFSETS = [(dz, dx) for dz in (-1, 0, 1) for dx in (-1, 0, 1)]


def split_np(x):
    x = np.asarray(x, np.float32)
    hi = x.astype(jnp.bfloat16)
    lo = (x - hi.astype(np.float32)).astype(jnp.bfloat16)
    return np.stack([hi, lo])


def half_rows(N):
    return -(-(N // 2 + 2) // 16) * 16


@functools.lru_cache(None)
def tables(G, S):
    MZ, MX, MY, N = G * BZ, S * BX, G * S, G * S
    p = np.arange(MY)
    ky = np.where(p <= MY // 2, p, p - MY // 2)
    ang = 2 * np.pi * ((ky[:, None] * np.arange(MY)[None, :]) % MY) / MY
    ct = np.where((p <= MY // 2)[:, None], np.cos(ang), np.sin(ang))
    kzl = np.repeat(np.arange(G), S)
    kxl = np.tile(np.arange(S), G)
    mate = (-kzl % G) * S + (-kxl % S)
    rows = np.arange(N)
    kept = rows[rows <= mate]
    count = np.where(kept == mate[kept], 1.0, 2.0)
    fill = half_rows(N) - len(kept)
    kept = np.concatenate([kept, np.zeros(fill, np.int64)])
    count = np.concatenate([count, np.zeros(fill)])
    rz, rx = kzl[kept], kxl[kept]
    ang = 2 * np.pi * (((rz[:, None] * kzl[None, :]) % G) / G + ((rx[:, None] * kxl[None, :]) % S) / S)
    w = np.concatenate([np.cos(ang), -np.sin(ang)], axis=0)
    a = np.repeat(np.arange(EZ), EX)
    b = np.tile(np.arange(EX), EZ)
    ang = 2 * np.pi * (rz[:, None] * (a - 1)[None] / MZ + rx[:, None] * (b - 1)[None] / MX)
    pad = ((0, 0), (0, ABP - EZ * EX))
    tw = np.stack([np.pad(np.cos(ang), pad), np.pad(-np.sin(ang), pad)]).astype(np.float32)
    kzh = np.repeat(np.arange(BZ), BX)
    kxh = np.tile(np.arange(BX), BZ)
    ang = 2 * np.pi * ((a - 1)[:, None] * kzh[None] / BZ + (b - 1)[:, None] * kxh[None] / BX)
    pad = ((0, ABP - EZ * EX), (0, 0))
    mr, mi = np.pad(np.cos(ang), pad), np.pad(-np.sin(ang), pad)
    fm = np.block([[mr, mi], [-mi, mr]])
    kz = rz[:, None] + G * kzh[None]
    kx = rx[:, None] + S * kxh[None]
    kz = kz - MZ * (2 * kz >= MZ)
    kx = kx - MX * (2 * kx >= MX)
    wave = (kz / (EDGE_LEN * G)) ** 2 + (kx / (EDGE_LEN * S)) ** 2
    scale = np.broadcast_to(count[:, None], wave.shape)
    gr = np.stack([wave, scale]).astype(np.float32)
    return split_np(ct), split_np(w), split_np(w.T), tw, split_np(fm), gr


def fit(fn, degree, top):
    z = top * (0.5 - 0.5 * np.cos(np.pi * (np.arange(200) + 0.5) / 200))
    return [float(c) for c in np.polynomial.polynomial.polyfit(z, fn(z), degree)]


COS_C = fit(lambda z: np.cos(np.pi * np.sqrt(z)), 6, 0.2526)
SIN_C = fit(lambda z: np.sin(np.pi * np.sqrt(z + 1e-300)) / np.sqrt(z + 1e-300), 5, 0.2526)


def poly(coefs, z):
    acc = jnp.full_like(z, coefs[-1])
    for c in coefs[-2::-1]:
        acc = acc * z + c
    return acc


def split(x):
    hi = x.astype(BF16)
    return hi, (x - hi.astype(F32)).astype(BF16)


def dg(a, b, dims):
    return lax.dot_general(a, b, (dims, ((), ())), preferred_element_type=F32)


NN = ((1,), (0,))
NT = ((1,), (1,))
TN = ((0,), (0,))


def dot3(a, b, dims):
    return dg(a[0], b[0], dims) + (dg(a[0], b[1], dims) + dg(a[1], b[0], dims))


def geometry(own, near, off_z, off_x, keep):
    dz = (off_z + near[0] - own[0]) * EDGE_LEN
    dx = (off_x + near[1] - own[1]) * EDGE_LEN
    dy = near[2] - own[2]
    dy = jnp.where(dy > 0.5, dy - 1.0, jnp.where(dy < -0.5, dy + 1.0, dy)) * PERIOD_Y
    rsq = dz * dz + dx * dx + dy * dy
    r2 = rsq + SOFTEN
    rinv = lax.rsqrt(r2)
    r = r2 * rinv
    x = jnp.minimum(r, 6.014) * (1.0 / CUTOFF) - 0.5
    z = x * x
    s1 = poly(COS_C, z)
    c1 = -x * poly(SIN_C, z)
    m = jnp.maximum(1.0 - rsq * (1.0 / (CUTOFF * CUTOFF)), 0.0) * keep
    env = m * m
    u = (dz * rinv, dx * rinv, dy * rinv)
    return rinv, s1, c1, m, env, u


def kernel(
    G, S,
    pos_hbm, feat_hbm, cnt_hbm, rw_hbm, mix_hbm, ow_hbm, cw_hbm, base_hbm, wts_hbm, slp_hbm,
    ct_hbm, w_hbm, wt_hbm, tw_hbm, fm_hbm, gr_hbm,
    e_out, f_out,
    pos_ref, feat_ref, cnt_ref, rw_ref, mix_ref, ow_ref, cw_ref, base_ref, wts_ref, slp_ref,
    ct, w, wt, tw, fm, gr,
    halo, hpos, posb, pv, wk, dk, uu_, radt, msg, gm, gp_a, gp_b, own_acc, ff, fr,
    ee, wzx, spec, plane, back, field, grn,
    in_sem, hs, hr, ps, pr_, fs, fr_sem, as_, ar, bs, br, ls, phase,
):
    N = G * S
    MY = N
    g = lax.axis_index("gz")
    s = lax.axis_index("xy")
    me = g * S + s

    def peer(dz, dx):
        return (lax.rem(g + (dz + G), G), lax.rem(s + (dx + S), S))

    loads = [pltpu.make_async_copy(h, v, in_sem.at[i]) for i, (h, v) in enumerate([
        (feat_hbm, feat_ref), (cnt_hbm, cnt_ref), (cw_hbm, cw_ref), (base_hbm, base_ref),
        (wts_hbm, wts_ref), (slp_hbm, slp_ref), (pos_hbm, pos_ref), (ct_hbm, ct),
        (rw_hbm, rw_ref), (mix_hbm, mix_ref), (ow_hbm, ow_ref),
        (w_hbm, w), (wt_hbm, wt), (tw_hbm, tw), (fm_hbm, fm), (gr_hbm, gr)])]
    for t in loads:
        t.start()

    bar = pltpu.get_barrier_semaphore()
    diag = [(dz, dx) for dz in (-1, 1) for dx in (-1, 1)]
    for dz, dx in diag:
        pl.semaphore_signal(bar, inc=1, device_id=peer(dz, dx), device_id_type=MESH)
    for dz in range(1, G):
        pl.semaphore_signal(bar, inc=1, device_id=peer(dz, 0), device_id_type=MESH)

    def sig_row(k, _):
        pl.semaphore_signal(bar, inc=1, device_id=(g, lax.rem(s + k, S)), device_id_type=MESH)
        return 0

    lax.fori_loop(1, S, sig_row, 0)

    for t in loads[:8]:
        t.wait()
    lane = lax.broadcasted_iota(jnp.int32, (1, T), 1)
    valid = (lane < cnt_ref[...]).astype(F32)
    featv = feat_ref[...].astype(F32) * valid
    halo[4] = jnp.transpose(featv)
    hpos[4] = jnp.concatenate([pos_ref[c] for c in range(3)] + [jnp.zeros((5, T), F32)], axis=0)
    cwt = jnp.transpose(jnp.broadcast_to(cw_ref[...], (8, F)))
    charge = jnp.sum(featv * cwt[:, 0:1], axis=0, keepdims=True)

    yrow = lax.broadcasted_iota(jnp.int32, (MY, T), 0)
    ty = jnp.bitwise_and(yrow - base_ref[2] + 1, MY - 1)
    wy = jnp.zeros((MY, T), F32)
    for c in range(4):
        wy = wy + jnp.where(ty == c, wts_ref[8 + c], 0.0)
    ab = lax.broadcasted_iota(jnp.int32, (ABP, T), 0)
    arow = lax.shift_right_logical(ab * 373, 12)
    brow = ab - arow * EX
    tz = arow - (base_ref[0] - g * BZ)
    tx = brow - (base_ref[1] - s * BX)
    zero = jnp.zeros((ABP, T), F32)
    wz, wx = zero, zero
    for c in range(4):
        wz = wz + jnp.where(tz == c, wts_ref[c], 0.0)
        wx = wx + jnp.where(tx == c, wts_ref[4 + c], 0.0)
    wzx[0] = wz * wx

    eh, el = split(dot3((ct[0], ct[1]), split(wy), NN))
    ee[0, :, :T] = eh
    ee[1, :, :T] = el
    spectrum = dot3((eh, el), split(wz * wx * charge), NT)
    spec[:, 0, :] = spectrum[:, :128]
    spec[:, 1, :] = spectrum[:, 128:]

    pl.semaphore_wait(bar, 4 + G - 1 + S - 1)

    def neighbour_copies(src, dst, send_sem, recv_sem, same_src):
        out = []
        for n, (dz, dx) in enumerate(OFFSETS):
            if n != 4:
                out.append(pltpu.make_async_remote_copy(
                    src_ref=src.at[4 if same_src else n], dst_ref=dst.at[8 - n],
                    send_sem=send_sem.at[n], recv_sem=recv_sem.at[8 - n],
                    device_id=peer(dz, dx), device_id_type=MESH))
        return out

    pos_copies = neighbour_copies(hpos, hpos, ps, pr_, True)
    for cp in pos_copies:
        cp.start()

    def feature_copy(src, dst, dz, dx):
        return pltpu.make_async_remote_copy(
            src_ref=halo.at[src], dst_ref=halo.at[dst], send_sem=hs.at[dst], recv_sem=hr.at[dst],
            device_id=peer(dz, dx), device_id_type=MESH)

    side_z = [feature_copy(4, 1, 1, 0), feature_copy(4, 7, -1, 0)]
    side_x = [feature_copy(4, 3, 0, 1), feature_copy(4, 5, 0, -1)]
    corners = [feature_copy(1, 0, 0, 1), feature_copy(1, 2, 0, -1),
               feature_copy(7, 6, 0, 1), feature_copy(7, 8, 0, -1)]
    for cp in side_z + side_x:
        cp.start()

    def sig_phase(k, _):
        pl.semaphore_signal(phase, inc=1, device_id=(g, lax.rem(s + k, S)), device_id_type=MESH)
        return 0

    lax.fori_loop(1, S, sig_phase, 0)
    own_t = jnp.transpose(hpos[4])
    for c in range(3):
        posb[c] = jnp.broadcast_to(own_t[:, c:c + 1], (T, T))

    lane_c = lax.broadcasted_iota(jnp.int32, (IC, T), 1)
    row_c = lax.broadcasted_iota(jnp.int32, (IC, T), 0)

    def pairs(n):
        off_z = (n // 3 - 1) * 1.0
        off_x = (lax.rem(n, 3) - 1) * 1.0
        near = [hpos[n, c:c + 1, :] for c in range(3)]

        def chunk(t, _):
            i0 = pl.multiple_of(t * IC, IC)
            rows = pl.ds(i0, IC)
            own = [posb[c, rows, :] for c in range(3)]
            same = jnp.logical_and(row_c + i0 == lane_c, n == 4)
            rinv, s1, c1, m, env, u = geometry(own, near, off_z, off_x, jnp.where(same, 0.0, 1.0))
            amp = env * rinv
            damp = -(m * (1.0 / 9.0) + env * (rinv * rinv))
            amp_r = amp * rinv
            amp_c = amp * (np.pi / CUTOFF)
            for c in range(3):
                uu_[n, c, rows, :] = u[c]
            two_c = 2.0 * c1
            s_prev, s_now = jnp.zeros_like(s1), s1
            c_prev, c_now = jnp.ones_like(c1), c1
            for k in range(K):
                lanes = slice(k * T, (k + 1) * T)
                e = s_now * amp
                pv[n, rows, lanes] = e.astype(BF16)
                for c in range(3):
                    pv[n, pl.ds((c + 1) * T + i0, IC), lanes] = (e * u[c]).astype(BF16)
                wk[n, k, rows, :] = s_now * amp_r
                dk[n, k, rows, :] = (c_now * float(k + 1)) * amp_c + s_now * damp
                s_prev, s_now = s_now, two_c * s_now - s_prev
                c_prev, c_now = c_now, two_c * c_now - c_prev
            return 0

        lax.fori_loop(0, T // IC, chunk, 0)

    pairs(jnp.int32(4))

    pl.semaphore_wait(phase, S - 1)

    def exchange(src, dst, send_sem, recv_sem):
        own = pltpu.make_async_copy(src.at[me], dst.at[me], ls)
        own.start()

        def one(j, dz):
            x2 = lax.bitwise_and((g // 2) + lax.bitwise_and(lax.shift_right_logical(0x36, 2 * (j // 8)), 3), 3)
            dy = lax.bitwise_and(lax.shift_right_logical(0x36, 2 * lax.rem(j // 2, 4)), 3)
            y2 = lax.bitwise_and(2 * lax.rem(g, 2) + lax.rem(s // 2, 2) + dy, 3)
            z2 = lax.bitwise_and(s // 4 + dz, 7)
            gq = 2 * x2 + y2 // 2
            sq = 4 * z2 + 2 * lax.rem(y2, 2) + lax.rem(s + j + 1, 2)
            pltpu.make_async_remote_copy(
                src_ref=src.at[gq * S + sq], dst_ref=dst.at[me], send_sem=send_sem, recv_sem=recv_sem,
                device_id=(gq, sq), device_id_type=MESH).start()

        def send(j, _):
            for dz in (4, 5, 3, 6, 2, 7, 1, 0):
                one(j, dz)
            return 0

        lax.fori_loop(0, 31, send, 0)
        for dz in (4, 5, 3, 6, 2, 7, 1):
            one(jnp.int32(31), dz)
        own.wait()

    def arrived(dst, sem):
        pltpu.make_async_copy(dst.at[pl.ds(0, N - 1)], dst.at[pl.ds(0, N - 1)], sem).wait()

    exchange(spec, plane, as_, ar)

    sy = jnp.zeros((MY, T), F32)
    for c in range(4):
        sy = sy + jnp.where(ty == c, slp_ref[8 + c], 0.0)
    eh, el = split(dot3((ct[0], ct[1]), split(sy), NN))
    ee[0, :, T:] = eh
    ee[1, :, T:] = el
    wz, sz, wx, sx = zero, zero, zero, zero
    for c in range(4):
        hit = tz == c
        wz = wz + jnp.where(hit, wts_ref[c], 0.0)
        sz = sz + jnp.where(hit, slp_ref[c], 0.0)
        hit = tx == c
        wx = wx + jnp.where(hit, wts_ref[4 + c], 0.0)
        sx = sx + jnp.where(hit, slp_ref[4 + c], 0.0)
    wzx[1] = sz * wx
    wzx[2] = wz * sx
    for t in loads[8:]:
        t.wait()
    ky = jnp.where(me <= MY // 2, me, me - MY // 2).astype(F32) * (1.0 / PERIOD_Y)
    twice = jnp.where(jnp.logical_or(me == 0, me == MY // 2), 1.0, 2.0)
    wsq = gr[0] + ky * ky
    positive = wsq > 0
    safe = jnp.where(positive, wsq, 1.0)
    green = COULOMB * jnp.exp(safe * (-np.pi ** 2 / EWALD_BETA ** 2)) / (
        (np.pi * EDGE_LEN * G * EDGE_LEN * S * PERIOD_Y) * safe)
    grn[...] = jnp.where(positive, green * twice, 0.0) * gr[1]

    for cp in pos_copies:
        cp.wait_recv()

    def pair_step(q, _):
        pairs(q + (q >= 4).astype(jnp.int32))
        return 0

    lax.fori_loop(0, 4, pair_step, 0)
    for cp in side_z:
        cp.wait_recv()
    for cp in corners:
        cp.start()
    lax.fori_loop(4, 8, pair_step, 0)

    msg[...] = jnp.zeros_like(msg)

    def forward(n):
        feat = halo[n]
        for k in range(K):
            radt[n, k * T:(k + 1) * T, :] = (feat * rw_ref[k:k + 1, :]).astype(BF16)
        msg[...] += dg(pv[n], radt[n], NN)
        return 0

    for cp in side_x:
        cp.wait_recv()
    forward(4)
    lax.fori_loop(0, 4, lambda q, _: forward(2 * q + 1), 0)

    arrived(plane, ar)
    rs = split(jnp.concatenate([plane[:, 0, :], plane[:, 1, :]], axis=1))
    y_all = dot3((w[0], w[1]), rs, NN)
    H = half_rows(N)
    yr, yi = y_all[:H], y_all[H:]
    tr, ti = tw[0], tw[1]
    yy = split(jnp.concatenate([tr * yr - ti * yi, tr * yi + ti * yr], axis=1))
    zz = dot3(yy, (fm[0], fm[1]), NN)
    zs = split(zz * jnp.concatenate([grn[...], grn[...]], axis=1))
    vv = dot3(zs, (fm[0], fm[1]), NT)
    vr, vi = vv[:, :ABP], vv[:, ABP:]
    vs = split(jnp.concatenate([tr * vr + ti * vi, tr * vi - ti * vr], axis=0))
    uu = dot3((wt[0], wt[1]), vs, NN)
    back[:, 0, :] = uu[:, :128]
    back[:, 1, :] = uu[:, 128:]
    exchange(back, field, bs, br)

    for cp in corners:
        cp.wait_recv()
    lax.fori_loop(0, 4, lambda q, _: forward(2 * q + 2 * (q >= 2).astype(jnp.int32)), 0)

    m0 = msg[0:T]
    mc = [msg[(c + 1) * T:(c + 2) * T] for c in range(3)]
    inv = (m0 + (mc[0] * mc[0] + mc[1] * mc[1] + mc[2] * mc[2])).astype(BF16)
    mix = mix_ref[...]
    pre = dg(inv, mix, NN)
    sig = 1.0 / (1.0 + jnp.exp(-pre))
    owr = ow_ref[...]
    energy_col = jnp.sum(pre * sig * owr, axis=1, keepdims=True)
    energy_sr = jnp.transpose(jnp.broadcast_to(energy_col, (T, T)))[0:1, :]
    valid_col = jnp.transpose(jnp.broadcast_to(valid, (8, T)))[:, 0:1]
    grad_pre = ((sig + pre * sig * (1.0 - sig)) * owr * valid_col).astype(BF16)
    grad_inv = dg(grad_pre, mix, NT)
    gm[0:T] = grad_inv.astype(BF16)
    for c in range(3):
        gm[(c + 1) * T:(c + 2) * T] = (2.0 * mc[c] * grad_inv).astype(BF16)

    own_acc[...] = jnp.zeros_like(own_acc)

    def grad_dot(n, gp):
        gp[...] = dg(gm[...], radt[n], NT)

    def grad_pairs(n, gp):
        near = [None] * 3
        for t in range(T // 8):
            rows = slice(t * 8, (t + 1) * 8)
            tc = [None] * 3
            bb = [None] * 4
            for k in range(K):
                lanes = slice(k * T, (k + 1) * T)
                wv, dv = wk[n, k, rows, :], dk[n, k, rows, :]
                for c in range(4):
                    v = gp[c * T + t * 8:c * T + (t + 1) * 8, lanes]
                    bb[c] = v * dv if k == 0 else bb[c] + v * dv
                    if c:
                        tc[c - 1] = v * wv if k == 0 else tc[c - 1] + v * wv
            u = [uu_[n, c, rows, :] for c in range(3)]
            b = bb[0]
            for c in range(3):
                b = b + u[c] * (bb[c + 1] - tc[c])
            for c in range(3):
                gr = tc[c] + u[c] * b
                own_acc[c, rows, :] += gr
                near[c] = gr if t == 0 else near[c] + gr
        for c in range(3):
            ff[n, c:c + 1, :] = -jnp.sum(near[c], axis=0, keepdims=True)

    ff[...] = jnp.zeros_like(ff)
    grad_dot(0, gp_a)

    def nth(q):
        return jnp.where(q == 8, 4, q + (q >= 4).astype(jnp.int32))

    def backward(t, _):
        grad_dot(nth(2 * t + 1), gp_b)
        grad_pairs(nth(2 * t), gp_a)
        grad_dot(nth(2 * t + 2), gp_a)
        grad_pairs(nth(2 * t + 1), gp_b)
        return 0

    lax.fori_loop(0, 4, backward, 0)

    force_copies = neighbour_copies(ff, fr, fs, fr_sem, False)
    for cp in force_copies:
        cp.start()
    grad_pairs(4, gp_a)

    arrived(field, br)
    phi = split(jnp.concatenate([field[:, 0, :], field[:, 1, :]], axis=1))
    along = dot3(phi, (ee[0], ee[1]), TN)
    a_w, a_s = along[:, :T], along[:, T:]
    pot = jnp.sum(a_w * wzx[0], axis=0, keepdims=True)
    rec = [
        -charge * jnp.sum(a_w * wzx[1], axis=0, keepdims=True),
        -charge * jnp.sum(a_w * wzx[2], axis=0, keepdims=True),
        -charge * jnp.sum(a_s * wzx[0], axis=0, keepdims=True),
    ]
    e_out[...] = valid * (energy_sr + 0.5 * charge * pot)
    own_rows = []
    for c in range(3):
        col = jnp.sum(own_acc[c], axis=1, keepdims=True)
        own_rows.append(jnp.transpose(jnp.broadcast_to(col, (T, T)))[0:1, :])

    for cp in force_copies:
        cp.wait_recv()
    near = ff[4]
    for n in range(9):
        if n != 4:
            near = near + fr[n]
    for c in range(3):
        f_out[c] = own_rows[c] + near[c:c + 1, :] + rec[c]
    for cp in pos_copies + side_z + side_x + corners + force_copies:
        cp.wait_send()
    arrived(spec, as_)
    arrived(back, bs)


def local(G, S, positions, features, cell_counts, radial_weights, mix_weights, out_weights,
          charge_weights, spline_base, spline_weights, spline_slopes):
    N = G * S
    H = half_rows(N)
    hbm = pl.BlockSpec(memory_space=pltpu.HBM)
    vm = pl.BlockSpec(memory_space=pltpu.VMEM)
    V = pltpu.VMEM
    DMA = pltpu.SemaphoreType.DMA
    e, f = pl.pallas_call(
        functools.partial(kernel, G, S),
        out_shape=(jax.ShapeDtypeStruct((1, T), F32), jax.ShapeDtypeStruct((3, 1, T), F32)),
        in_specs=[hbm] * 16,
        out_specs=[vm, vm],
        scratch_shapes=[
            V((3, 1, T), F32), V((F, T), BF16), V((1, 1), jnp.int32), V((K, F), F32), V((F, F), BF16),
            V((1, F), F32), V((1, F), F32), V((3, 1, T), jnp.int32), V((12, 1, T), F32), V((12, 1, T), F32),
            V((2, N, N), BF16), V((2, 2 * H, N), BF16), V((2, N, 2 * H), BF16), V((2, H, ABP), F32), V((2, 2 * ABP, 256), BF16),
            V((2, H, 128), F32),
            V((9, T, F), F32), V((9, 8, T), F32), V((3, T, T), F32), V((9, 4 * T, K * T), BF16),
            V((9, K, T, T), F32), V((9, K, T, T), F32), V((9, 3, T, T), F32), V((9, K * T, F), BF16),
            V((4 * T, F), F32), V((4 * T, F), BF16), V((4 * T, K * T), F32), V((4 * T, K * T), F32),
            V((3, T, T), F32), V((9, 8, T), F32), V((9, 8, T), F32),
            V((2, N, 2 * T), BF16), V((3, ABP, T), F32),
            V((N, 2, 128), F32), V((N, 2, 128), F32), V((N, 2, 128), F32), V((N, 2, 128), F32),
            V((H, 128), F32),
            DMA((16,)), DMA((9,)), DMA((9,)), DMA((9,)), DMA((9,)), DMA((9,)), DMA((9,)),
            DMA, DMA, DMA, DMA, DMA, pltpu.SemaphoreType.REGULAR,
        ],
        compiler_params=pltpu.CompilerParams(collective_id=0, has_side_effects=True,
                                             vmem_limit_bytes=60 * 1024 * 1024),
    )(
        positions.reshape(3, 1, T), features.reshape(F, T), cell_counts, radial_weights, mix_weights,
        out_weights.reshape(1, F), charge_weights.reshape(1, F), spline_base.reshape(3, 1, T),
        spline_weights.reshape(12, 1, T), spline_slopes.reshape(12, 1, T),
        *[jnp.asarray(t) for t in tables(G, S)],
    )
    return e.reshape(1, 1, T), f.reshape(3, 1, 1, T)


def solution(mesh):
    placed = (
        P(None, "gz", "xy", None), P(None, "gz", "xy", None), P("gz", "xy"), P(), P(), P(), P(),
        P(None, "gz", "xy", None), P(None, None, "gz", "xy", None), P(None, None, "gz", "xy", None),
    )
    return jax.shard_map(
        functools.partial(local, mesh.shape["gz"], mesh.shape["xy"]),
        mesh=mesh, in_specs=placed,
        out_specs=(P("gz", "xy", None), P(None, "gz", "xy", None)),
        check_vma=False,
    )
```
